32 devices in a mesh: grp: 4 (over x, core), row: 8 (over z, y).
Axes of the slice: x: 2, y: 2, z: 4, core: 2. Of those that a mesh axis runs over, the one named last changes fastest.
Arguments:
- features: bfloat16 [2048, 4096], P('row', 'grp'), may hold values from -0.125 to 0.125
- residual: float32 [2048, 576], P('row'), may hold values from -6 to 6
- precond: float32 [4096, 1024], P('grp'), as said below
Outputs:
- coefs: float32 [4096, 576], P('grp')
- section_resid: float32 [4, 2048, 576], P('grp', 'row')
The draws below stay inside these ranges and needn't reach their ends.
Inputs may be any that keep to these rules, and one draw needn't show every extreme that they name: Each 1024 x 1024 block of precond is symmetric and positive definite.
All inputs are finite; a program needn't handle non-finite values.
Results may differ from the reference program's by a relative error of at most 0.009.
Values may be sent and summed in bfloat16 or wider, within the bound.
No kernel may reach another device: no remote copies, remote signals or barrier semaphores. Data moves between devices by JAX's collectives and lax.ppermute only.
A program may use at most 64 MiB of HBM per device.

```python
import jax
import jax.numpy as jnp
from jax import lax

BLK = 1024
TGT = 576
ROWS = 2048
NBLK = 4


def draw_precond(key, part):
    first_key = jax.random.fold_in(jax.random.fold_in(key, 11), 0)
    noise = jax.random.normal(first_key, (NBLK, BLK, BLK), jnp.float32)
    scales = jnp.ones((NBLK, BLK), jnp.float32)
    symmetric = (noise + jnp.swapaxes(noise, 1, 2)) / jnp.sqrt(2.0)
    matrix = jnp.eye(BLK, dtype=jnp.float32)[None] + symmetric * (0.3 / jnp.sqrt(float(BLK)))
    roots = jnp.sqrt(scales)
    matrix = roots[:, :, None] * matrix * roots[:, None, :]
    return matrix.reshape(NBLK * BLK, BLK)


def block_scale(key, dims, cuts, least, largest):
    factor_of = 1.0
    for dim, blocks in cuts:
        heights = jax.random.uniform(jax.random.fold_in(jax.random.fold_in(key, 6), dim), (blocks,), jnp.float32, least / len(cuts), largest / len(cuts))
        factor_of = factor_of * jnp.repeat(jnp.exp(heights), dims[dim] // blocks).reshape((-1,) + (1,) * (len(dims) - 1 - dim))
    return factor_of


def centred(rng, shape, spread, bound, shards=(), kind=jnp.bfloat16):
    level = block_scale(rng, shape, shards, -0.22, 0.18) if shards else 1.0
    result = jax.random.normal(rng, shape, jnp.float32) * spread * level
    return jnp.minimum(jnp.maximum(result, -bound), bound).astype(kind)


def setup_inputs(seed: int = 0) -> dict:
    splits = jax.random.split(jax.random.key(seed), 4)
    features = centred(splits[0], (ROWS, NBLK * BLK), ROWS ** -0.5, 0.125, ((0, 8), (1, 4)))
    residual = centred(splits[1], (ROWS, TGT), 1.0, 6.0, ((0, 8),), jnp.float32)
    precond = draw_precond(jax.random.fold_in(splits[3], 71), 0)
    return dict(features=features, residual=residual, precond=precond)


def reference(features, residual, precond):
    remaining = residual
    coef_list = []
    resid_list = []
    for block_index in range(NBLK):
        block = features[:, block_index * BLK:(block_index + 1) * BLK]
        block_map = precond[block_index * BLK:(block_index + 1) * BLK]
        rounded = remaining.astype(jnp.bfloat16)
        correlation = lax.dot_general(block, rounded, (((0,), (0,)), ((), ())), preferred_element_type=jnp.float32)
        coefficient = jnp.dot(block_map, correlation, precision=lax.Precision.HIGHEST)
        remaining = remaining - jnp.dot(block, coefficient.astype(jnp.bfloat16), preferred_element_type=jnp.float32)
        coef_list.append(coefficient)
        resid_list.append(remaining)
    return jnp.concatenate(coef_list, axis=0), jnp.stack(resid_list, axis=0)
```

```python
import functools

import jax
import jax.numpy as jnp
from jax import lax
from jax.experimental import pallas as pl
from jax.experimental.pallas import tpu as pltpu
from jax.sharding import PartitionSpec as P

F32 = jnp.float32
BF16 = jnp.bfloat16
CORES = 2
PAIR = 2
ANY = pl.BlockSpec(memory_space=pl.ANY)
VMEM = pl.BlockSpec(memory_space=pltpu.VMEM)
SMEM = pl.BlockSpec(memory_space=pltpu.SMEM)


def pick_copy(use_own, own, other, dst, sem):
    @pl.when(use_own)
    def _():
        pltpu.make_async_copy(own, dst, sem).start()

    @pl.when(jnp.logical_not(use_own))
    def _():
        pltpu.make_async_copy(other, dst, sem).start()

    return pltpu.make_async_copy(own, dst, sem).wait


def correlate_into(r_ref, rows, waits, blocks, c_ref):
    total = None
    for q, wait in enumerate(waits):
        wait()
        part = jnp.dot(
            r_ref[:, q * rows:(q + 1) * rows].astype(BF16),
            blocks[q],
            preferred_element_type=F32,
        )
        total = part if total is None else total + part
    c_ref[...] = total.astype(BF16)


def first_kernel(count, mine_ref, r_ref, *refs):
    own, other = refs[:count], refs[count:2 * count]
    c_ref, blocks, sems = refs[2 * count:]
    use_own = mine_ref[0] == 1
    waits = [pick_copy(use_own, own[q], other[q], blocks.at[q], sems.at[q]) for q in range(count)]
    correlate_into(r_ref, own[0].shape[0], waits, blocks, c_ref)


def stage_kernel(count, has_next, mine_ref, r_ref, ca_ref, cb_ref, *refs):
    own, other = refs[:count], refs[count:2 * count]
    maps = refs[2 * count:2 * count + 4]
    outs = refs[2 * count + 4:]
    if has_next:
        w_ref, rn_ref, rb_ref, cn_ref, blocks, upper, lower, nexts, sems, map_sems, next_sems = outs
    else:
        w_ref, rn_ref, rb_ref, blocks, upper, lower, sems, map_sems = outs
    use_own = mine_ref[0] == 1
    map_waits = [
        pick_copy(use_own, maps[0], maps[1], upper, map_sems.at[0]),
        pick_copy(use_own, maps[2], maps[3], lower, map_sems.at[1]),
    ]
    waits = [pick_copy(use_own, own[q], other[q], blocks.at[q], sems.at[q]) for q in range(count)]
    if has_next:
        next_waits = [
            pick_copy(use_own, other[q], own[q], nexts.at[q], next_sems.at[q]) for q in range(count)
        ]
    rows = own[0].shape[0]
    total = ca_ref[...].astype(F32) + cb_ref[...].astype(F32)
    high = total.astype(BF16)
    low = (total - high.astype(F32)).astype(BF16)
    map_waits[0]()
    w = jnp.dot(high, upper[...], preferred_element_type=F32)
    w += jnp.dot(low, upper[...], preferred_element_type=F32)
    map_waits[1]()
    w += jnp.dot(high, lower[...], preferred_element_type=F32)
    wb = w.astype(BF16)
    w_ref[...] = wb
    for q in range(count):
        waits[q]()
        span = pl.ds(q * rows, rows)
        fresh = r_ref[:, span] - lax.dot_general(
            wb, blocks[q], (((1,), (1,)), ((), ())), preferred_element_type=F32
        )
        rn_ref[:, span] = fresh
        rb_ref[:, span] = fresh.astype(BF16)
    if has_next:
        correlate_into(rn_ref, rows, next_waits, nexts, cn_ref)


def first_call(mine, panel, own, other):
    count = len(own)
    rows, feats = own[0].shape
    width = panel.shape[0]
    return pl.pallas_call(
        functools.partial(first_kernel, count),
        out_shape=jax.ShapeDtypeStruct((width, feats), BF16),
        in_specs=[SMEM, VMEM] + [ANY] * (2 * count),
        out_specs=VMEM,
        scratch_shapes=[pltpu.VMEM((count, rows, feats), BF16), pltpu.SemaphoreType.DMA((count,))],
        cost_estimate=pl.CostEstimate(
            flops=2 * width * rows * count * feats, bytes_accessed=2 * rows * count * feats, transcendentals=0
        ),
        name="first_corr",
    )(mine, panel, *own, *other)


def stage_call(mine, panel, ca, cb, own, other, maps, has_next):
    count = len(own)
    rows, feats = own[0].shape
    width = panel.shape[0]
    wide = jax.ShapeDtypeStruct((width, feats), BF16)
    out_shape = [
        wide,
        jax.ShapeDtypeStruct(panel.shape, F32),
        jax.ShapeDtypeStruct(panel.shape, BF16),
    ]
    scratch = [
        pltpu.VMEM((count, rows, feats), BF16),
        pltpu.VMEM((feats, feats), BF16),
        pltpu.VMEM((feats, feats), BF16),
    ]
    sems = [pltpu.SemaphoreType.DMA((count,)), pltpu.SemaphoreType.DMA((2,))]
    if has_next:
        out_shape.append(wide)
        scratch.append(pltpu.VMEM((count, rows, feats), BF16))
        sems.append(pltpu.SemaphoreType.DMA((count,)))
    return pl.pallas_call(
        functools.partial(stage_kernel, count, has_next),
        out_shape=out_shape,
        in_specs=[SMEM] + [VMEM] * 3 + [ANY] * (2 * count + 4),
        out_specs=[VMEM] * len(out_shape),
        scratch_shapes=scratch + sems,
        cost_estimate=pl.CostEstimate(
            flops=2 * width * feats * (3 * feats + (1 + has_next) * rows * count),
            bytes_accessed=2 * feats * (2 * feats + (1 + has_next) * rows * count),
            transcendentals=0,
        ),
        name="sweep_stage",
    )(mine, panel, ca, cb, *own, *other, *maps)


def sweep(features, residual, precond):
    grp_count, row_count = lax.axis_size("grp"), lax.axis_size("row")
    g, r = lax.axis_index("grp"), lax.axis_index("row")
    core = g % CORES
    plane = g // CORES
    plane_count = grp_count // CORES
    rows, feats = features.shape
    targets = residual.shape[1]
    panel_count = row_count // PAIR * CORES
    width = targets // panel_count

    def permute(x, mask=0, flip=0, keep=None, shift=0):
        route = []
        for a in range(grp_count):
            if keep is not None and a % CORES != keep:
                continue
            b = (a ^ flip) + shift
            if b >= grp_count:
                continue
            for i in range(row_count):
                route.append((a * row_count + i, b * row_count + (i ^ mask)))
        return lax.ppermute(x, ("grp", "row"), route)

    bits = [1 << i for i in range(row_count.bit_length() - 1) if (1 << i) != PAIR]
    masks = [0]
    for bit in reversed(bits):
        masks += [m ^ bit for m in masks]

    def place_of(index):
        return (index // (2 * PAIR)) * PAIR + index % PAIR

    own = {0: features}
    for bit in reversed(bits):
        for m in list(own):
            own[m ^ bit] = permute(own[m], mask=bit)
    own = [own[m] for m in masks]
    upper = precond.astype(BF16)
    lower = (precond - upper.astype(F32)).astype(BF16)
    upper_other = permute(upper, flip=1)
    lower_other = permute(lower, flip=1)
    maps = (upper, upper_other, lower, lower_other)
    other = [permute(a, flip=1) for a in own]

    turned = residual.T

    def slice_for(mask):
        at = (place_of(r ^ mask) * CORES + core) * width
        return lax.dynamic_slice_in_dim(turned, at, width, 0)

    panel = jnp.concatenate(
        [slice_for(0)] + [permute(slice_for(m), mask=m) for m in masks[1:]], axis=1
    )

    first_mine = jnp.where(core == 0, 1, 0).astype(jnp.int32).reshape(1)
    second_mine = 1 - first_mine
    maps_swap = maps

    keep_first = keep_second = base = None
    passed = None
    for step in range(plane_count):
        here = plane == step
        corr = first_call(first_mine, panel, own, other)
        w1, panel1, _, corr = stage_call(
            first_mine, panel, corr, permute(corr, mask=PAIR), own, other, maps, True
        )[0:4]
        w2, _, panel2 = stage_call(
            second_mine, panel1, corr, permute(corr, mask=PAIR), own, other, maps_swap, False
        )
        keep_first = w1 if keep_first is None else jnp.where(here, w1, keep_first)
        keep_second = w2 if keep_second is None else jnp.where(here, w2, keep_second)
        if step + 1 < plane_count:
            moved = permute(panel2, shift=CORES)
            passed = moved if passed is None else jnp.where(plane == step + 1, moved, passed)
            panel = moved.astype(F32)

    def gather(kept, which):
        sent = permute(kept, flip=1, keep=1 - which)
        pair = jnp.concatenate((kept, sent) if which == 0 else (sent, kept), axis=0)
        held = {0: pair}
        for bit in reversed(bits):
            for m in list(held):
                held[m ^ bit] = permute(held[m], mask=bit, keep=which)
        return [held[m] for m in masks]

    first_parts = gather(keep_first, 0)
    second_parts = gather(keep_second, 1)
    coef_t = jnp.zeros((targets, feats), BF16)
    for m, a, b in zip(masks, first_parts, second_parts):
        part = jnp.where(core == 0, a, b)
        coef_t = lax.dynamic_update_slice_in_dim(coef_t, part, place_of(r ^ m) * CORES * width, 0)

    base_t = turned
    if passed is not None:
        sibling = permute(passed, flip=1)
        pair = jnp.where(
            core == 0,
            jnp.concatenate((passed, sibling), axis=0),
            jnp.concatenate((sibling, passed), axis=0),
        )
        for k, m in enumerate(masks):
            block = pair[:, k * rows:(k + 1) * rows]
            block = permute(block, mask=m) if m else block
            start = place_of(r ^ m) * CORES * width
            old = lax.dynamic_slice_in_dim(turned, start, CORES * width, 0)
            base_t = lax.dynamic_update_slice_in_dim(
                base_t, jnp.where(plane == 0, old, block.astype(F32)), start, 0
            )
    change_t = lax.dot_general(
        coef_t, features, (((1,), (1,)), ((), ())), preferred_element_type=F32
    )
    after_t = base_t - change_t
    before_t = permute(after_t, flip=1, keep=0)
    resid_t = jnp.where(core == 0, after_t, before_t - change_t)
    return coef_t.T.astype(F32), resid_t.T[None]


def solution(mesh):
    placed = (P("row", "grp"), P("row", None), P("grp", None))
    return jax.shard_map(
        sweep,
        mesh=mesh,
        in_specs=placed,
        out_specs=(P("grp", None), P("grp", "row", None)),
        check_vma=False,
    )
```

```python
import functools

import jax
import jax.numpy as jnp
from jax import lax
from jax.experimental import pallas as pl
from jax.experimental.pallas import tpu as pltpu
from jax.sharding import PartitionSpec as P


F32 = jnp.float32
BF16 = jnp.bfloat16
CORES = 2
PAIR = 2
VMEM = pl.BlockSpec(memory_space=pltpu.VMEM)
GRANT = 24 * 1024 * 1024


def correlation(r_ref, blocks, c_ref):
    rows = blocks[0].shape[0]
    total = None
    for q, block in enumerate(blocks):
        part = jnp.dot(
            r_ref[:, q * rows:(q + 1) * rows].astype(BF16), block[...], preferred_element_type=F32
        )
        total = part if total is None else total + part
    c_ref[...] = total.astype(BF16)


def first_kernel(count, r_ref, *refs):
    correlation(r_ref, refs[:count], refs[count])


def stage_kernel(count, r_ref, ca_ref, cb_ref, map_ref, *refs):
    blocks = refs[:count]
    w_ref, rn_ref = refs[count:]
    rows = blocks[0].shape[0]
    width = ca_ref.shape[0]
    total = ca_ref[...].astype(F32) + cb_ref[...].astype(F32)
    high = total.astype(BF16)
    low = (total - high.astype(F32)).astype(BF16)
    both = jnp.dot(jnp.concatenate((high, low), axis=0), map_ref[...], preferred_element_type=F32)
    wb = (both[:width] + both[width:]).astype(BF16)
    w_ref[...] = wb
    for q in range(count):
        span = pl.ds(q * rows, rows)
        fresh = r_ref[:, span].astype(F32) - lax.dot_general(
            wb, blocks[q][...], (((1,), (1,)), ((), ())), preferred_element_type=F32
        )
        rn_ref[:, span] = fresh.astype(rn_ref.dtype)


def final_kernel(count, info_ref, a_ref, before_ref, after_ref, *refs):
    first, second = refs[:count], refs[count:2 * count]
    coef_ref, resid_ref = refs[2 * count:]
    height = first[0].shape[0]

    def place(q):
        return pl.ds(pl.multiple_of(info_ref[1 + q], 8), height)

    @pl.when(info_ref[0] == 1)
    def _():
        for q in range(count):
            coef_ref[place(q), :] = first[q][...].astype(F32)
        resid_ref[...] = after_ref[...]

    @pl.when(info_ref[0] == 0)
    def _():
        for q in range(count):
            part = second[q][...]
            coef_ref[place(q), :] = part.astype(F32)
            resid_ref[place(q), :] = before_ref[place(q), :] - lax.dot_general(
                part, a_ref[...], (((1,), (1,)), ((), ())), preferred_element_type=F32
            )


def update_kernel(count, info_ref, a_ref, base_ref, *refs):
    parts, out_ref = refs[:count], refs[count]
    height = parts[0].shape[0]
    for q in range(count):
        at = pl.ds(pl.multiple_of(info_ref[1 + q], 8), height)
        out_ref[at, :] = base_ref[at, :] - lax.dot_general(
            parts[q][...], a_ref[...], (((1,), (1,)), ((), ())), preferred_element_type=F32
        )


def base_kernel(count, info_ref, turned_ref, *refs):
    parts, out_ref = refs[:count], refs[count]
    height = parts[0].shape[0]

    @pl.when(info_ref[1 + count] == 1)
    def _():
        out_ref[...] = turned_ref[...]

    @pl.when(info_ref[1 + count] == 0)
    def _():
        for q in range(count):
            at = pl.ds(pl.multiple_of(info_ref[1 + q], 8), height)
            out_ref[at, :] = parts[q][...].astype(F32)


def local_call(body, out_shape, info, arrays):
    many = isinstance(out_shape, (list, tuple))
    return pl.pallas_call(
        body,
        out_shape=out_shape,
        in_specs=[pl.BlockSpec(memory_space=pltpu.SMEM)] + [VMEM] * len(arrays),
        out_specs=[VMEM] * len(out_shape) if many else VMEM,
        compiler_params=pltpu.CompilerParams(vmem_limit_bytes=GRANT),
    )(info, *arrays)


def first_call(panel, blocks):
    count = len(blocks)
    rows, feats = blocks[0].shape
    width = panel.shape[0]
    return pl.pallas_call(
        functools.partial(first_kernel, count),
        out_shape=jax.ShapeDtypeStruct((width, feats), BF16),
        in_specs=[VMEM] * (1 + count),
        out_specs=VMEM,
        cost_estimate=pl.CostEstimate(
            flops=2 * width * rows * count * feats, bytes_accessed=2 * rows * count * feats, transcendentals=0
        ),
        compiler_params=pltpu.CompilerParams(vmem_limit_bytes=GRANT),
        name="first_corr",
    )(panel, *blocks)


def stage_call(panel, ca, cb, square, blocks, kind):
    count = len(blocks)
    rows, feats = blocks[0].shape
    width = panel.shape[0]
    return pl.pallas_call(
        functools.partial(stage_kernel, count),
        out_shape=[jax.ShapeDtypeStruct((width, feats), BF16), jax.ShapeDtypeStruct(panel.shape, kind)],
        in_specs=[VMEM] * (4 + count),
        out_specs=[VMEM] * 2,
        cost_estimate=pl.CostEstimate(
            flops=2 * width * feats * (2 * feats + rows * count),
            bytes_accessed=2 * feats * (feats + rows * count),
            transcendentals=0,
        ),
        compiler_params=pltpu.CompilerParams(vmem_limit_bytes=GRANT),
        name="sweep_stage",
    )(panel, ca, cb, square, *blocks)


def sweep(features, residual, precond):
    grp_count, row_count = lax.axis_size("grp"), lax.axis_size("row")
    g, r = lax.axis_index("grp"), lax.axis_index("row")
    core = g % CORES
    plane = g // CORES
    plane_count = grp_count // CORES
    rows, feats = features.shape
    targets = residual.shape[1]
    panel_count = row_count // PAIR * CORES
    width = targets // panel_count

    def permute(x, mask=0, flip=0, keep=None, shift=0):
        route = []
        for a in range(grp_count):
            if keep is not None and a % CORES != keep:
                continue
            b = (a ^ flip) + shift
            if b >= grp_count:
                continue
            for i in range(row_count):
                route.append((a * row_count + i, b * row_count + (i ^ mask)))
        return lax.ppermute(x, ("grp", "row"), route)

    bits = [1 << i for i in range(row_count.bit_length() - 1) if (1 << i) != PAIR]
    masks = [0]
    for bit in reversed(bits):
        masks += [m ^ bit for m in masks]

    def place_of(index):
        return (index // (2 * PAIR)) * PAIR + index % PAIR

    def after(x, *others):
        return lax.optimization_barrier((x,) + others)[0]

    info = jnp.stack(
        [jnp.where(core == 0, 1, 0)]
        + [place_of(r ^ m) * CORES * width for m in masks]
        + [jnp.where(plane == 0, 1, 0)]
    ).astype(jnp.int32)
    starts = [((place_of(r ^ m) * CORES + core) * width).astype(jnp.uint32) for m in masks]
    on_first = core == 0
    at_plane = [plane == step for step in range(plane_count)]
    features, info, starts, on_first, at_plane = lax.optimization_barrier(
        (features, info, starts, on_first, at_plane)
    )
    on_second = jnp.logical_not(on_first)
    far = bits[-1]

    near = bits[:-1]
    first_held = {0: features, far: permute(features, mask=far, keep=0)}
    for bit in reversed(near):
        first_held[bit] = permute(features, mask=bit, keep=0)
    swapped = permute(features, flip=1)
    square = after(precond, swapped).astype(BF16)
    square_swapped = permute(square, flip=1)
    first_square = jnp.where(on_first, square, square_swapped)
    second_square = jnp.where(on_first, square_swapped, square)

    def on_both(x, which):
        mine = on_first if which == 0 else on_second
        return jnp.where(mine, x, permute(x, flip=1, keep=which))

    first_blocks = {0: jnp.where(on_first, features, swapped)}
    second_blocks = {0: jnp.where(on_second, features, swapped)}
    for bit in near:
        first_blocks[bit] = on_both(first_held[bit], 0)

    turned = residual.T
    zero = jnp.uint32(0)

    def slice_for(k):
        return lax.dynamic_slice(turned, (starts[k], zero), (width, rows))

    slices = [slice_for(k).astype(BF16) if m else slice_for(k) for k, m in enumerate(masks)]

    first_held[far], first_square, second_square, first_blocks, second_blocks, slices = (
        lax.optimization_barrier(
            (first_held[far], first_square, second_square, first_blocks, second_blocks, slices)
        )
    )
    for bit in reversed(near):
        for m in [m for m in masks if m and m not in first_held and (m ^ bit) in first_held]:
            first_held[m] = permute(first_held[m ^ bit], mask=bit, keep=0)
    second_held = {0: features, far: permute(after(features, first_held[far]), mask=far, keep=1)}
    for bit in reversed(near):
        second_held[bit] = permute(after(features, first_held[bit]), mask=bit, keep=1)
    moved = [permute(x, mask=m) for x, m in zip(slices, masks) if m]
    panel = jnp.concatenate([slices[0]] + [x.astype(F32) for x in moved], axis=1)
    for m in masks:
        if m not in first_blocks:
            first_blocks[m] = on_both(first_held[m], 0)
    first_blocks = [first_blocks[m] for m in masks]

    keep_first = keep_second = passed = blocks = None
    count = len(masks)
    for step in range(plane_count):
        end = step + 1 == plane_count
        corr = first_call(panel, first_blocks)
        if step == 0:
            for m in [far] + near:
                second_held[m] = after(second_held[m], corr)
            for bit in reversed(near):
                for m in [m for m in masks if m not in second_held and (m ^ bit) in second_held]:
                    second_held[m] = permute(second_held[m ^ bit], mask=bit, keep=1)
            for m in masks[1:]:
                second_blocks[m] = on_both(second_held[m], 1)
            second_blocks = [second_blocks[m] for m in masks]
        got = permute(corr, mask=PAIR)
        if end and passed is not None:
            sibling = permute(after(passed, corr), flip=1)
            got = after(got, sibling)
            pair = jnp.concatenate(
                (jnp.where(on_first, passed, sibling), jnp.where(on_first, sibling, passed)), axis=0
            )
            blocks = [pair[:, k * rows:(k + 1) * rows] for k in range(count)]
            blocks = [permute(x, mask=m) if m else x for x, m in zip(blocks, masks)]
        w1, panel1 = stage_call(panel, corr, got, first_square, first_blocks, F32)
        keep_first = w1 if keep_first is None else jnp.where(at_plane[step], w1, keep_first)
        corr = first_call(panel1, second_blocks)
        got = permute(corr, mask=PAIR)
        if end:
            sent = permute(after(keep_first, corr), flip=1, keep=1)
            got = after(got, sent)
        w2, panel2 = stage_call(panel1, corr, got, second_square, second_blocks, BF16)
        keep_second = w2 if keep_second is None else jnp.where(at_plane[step], w2, keep_second)
        if not end:
            panel = permute(panel2, shift=CORES)
            passed = panel if passed is None else jnp.where(at_plane[step + 1], panel, passed)

    def gather(pair, which):
        held = {0: pair}
        for bit in reversed(bits):
            for m in list(held):
                held[m ^ bit] = permute(held[m], mask=bit, keep=which)
        return [held[m] for m in masks]

    first_parts = gather(jnp.concatenate((keep_first, sent), axis=0), 0)
    sent = permute(keep_second, flip=1, keep=0)
    second_parts = gather(jnp.concatenate((sent, keep_second), axis=0), 1)

    whole = jax.ShapeDtypeStruct((targets, rows), F32)
    base = turned
    if blocks is not None:
        base = local_call(functools.partial(base_kernel, count), whole, info, [turned] + blocks)
    after_first = local_call(functools.partial(update_kernel, count), whole, info, [features, base] + first_parts)
    before_second = permute(after_first, flip=1, keep=0)
    coef_t, resid_t = local_call(
        functools.partial(final_kernel, count),
        [jax.ShapeDtypeStruct((targets, feats), F32), whole],
        info,
        [features, before_second, after_first] + first_parts + second_parts,
    )
    return coef_t.T, resid_t.T[None]


def solution(mesh):
    placed = (P("row", "grp"), P("row", None), P("grp", None))

    return jax.shard_map(
        sweep,
        mesh=mesh,
        in_specs=placed,
        out_specs=(P("grp", None), P("grp", "row", None)),
        check_vma=False,
    )
```

```python
import functools

import jax
import jax.numpy as jnp
from jax import lax
from jax.experimental import pallas as pl
from jax.experimental.pallas import tpu as pltpu
from jax.sharding import PartitionSpec as P


F32 = jnp.float32
BF16 = jnp.bfloat16
CORES = 2
PAIR = 2
TILE = 8
VMEM = pl.BlockSpec(memory_space=pltpu.VMEM)
SCALARS = pl.BlockSpec(memory_space=pltpu.SMEM)
GRANT = 24 * 1024 * 1024


def grouped(refs, layout):
    out, at = [], 0
    for size in layout:
        out.append(refs[at:at + size])
        at += size
    return out


def correlation(r_ref, blocks, c_ref):
    rows, feats = blocks[0][0].shape[0], c_ref.shape[1]
    cut = feats // 2
    whole = [(q, b[0]) for q, b in enumerate(blocks) if len(b) == 1]
    split = [(q, b) for q, b in enumerate(blocks) if len(b) == 2]
    lhs = [r_ref[:, q * rows:(q + 1) * rows].astype(BF16) for q in range(len(blocks))]
    for k in range(2):
        span = pl.ds(k * cut, cut)
        total = None
        for q, block in whole:
            part = jnp.dot(lhs[q], block[:, span], preferred_element_type=F32)
            total = part if total is None else total + part
        for q, block in split:
            total += jnp.dot(lhs[q], block[k][...], preferred_element_type=F32)
        c_ref[:, span] = total.astype(BF16)


def core_is(index):
    return lax.axis_index("grp") % CORES == index


def first_kernel(layout, owner, r_ref, *refs):
    count = sum(layout)

    @pl.when(core_is(owner))
    def _():
        correlation(r_ref, grouped(refs[:count], layout), refs[2 * count])

    @pl.when(core_is(1 - owner))
    def _():
        correlation(r_ref, grouped(refs[count:2 * count], layout), refs[2 * count])


def stage_kernel(layout, owner, r_ref, ca_ref, cb_ref, own_ref, other_ref, *refs):
    count = sum(layout)
    w_ref, rn_ref = refs[2 * count:]
    width = ca_ref.shape[0]
    total = ca_ref[...].astype(F32) + cb_ref[...].astype(F32)
    high = total.astype(BF16)
    low = (total - high.astype(F32)).astype(BF16)
    stacked = jnp.concatenate((high, low), axis=0)

    def run(map_ref, blocks):
        both = jnp.dot(stacked, map_ref[...], preferred_element_type=F32)
        wb = (both[:width] + both[width:]).astype(BF16)
        w_ref[...] = wb
        rows = blocks[0][0].shape[0]
        cut = wb.shape[1] // 2
        for q, block in enumerate(blocks):
            span = pl.ds(q * rows, rows)
            if len(block) == 1:
                change = product(wb, block[0])
            else:
                change = product(wb[:, :cut], block[0]) + product(wb[:, cut:], block[1])
            rn_ref[:, span] = (r_ref[:, span].astype(F32) - change).astype(rn_ref.dtype)

    @pl.when(core_is(owner))
    def _():
        run(own_ref, grouped(refs[:count], layout))

    @pl.when(core_is(1 - owner))
    def _():
        run(other_ref, grouped(refs[count:2 * count], layout))


def product(w, a_ref):
    return lax.dot_general(w, a_ref[...], (((1,), (1,)), ((), ())), preferred_element_type=F32)


def spans(info_ref, count, height):
    if height % TILE:
        return [pl.ds(q * height, height) for q in range(count)]
    return [pl.ds(pl.multiple_of(info_ref[q], TILE), height) for q in range(count)]


def rows_of(ref, q, height):
    return ref[q * height:(q + 1) * height, :]


def both_panels(first_core, own, got):
    return jnp.concatenate((own, got) if first_core else (got, own), axis=0)


def update_kernel(count, info_ref, own_ref, other_ref, base_ref, got_ref, *refs):
    parts, out_ref = refs[:count], refs[count]
    height = parts[0].shape[0]

    def run(first_core, a_ref):
        for q, at in enumerate(spans(info_ref, count, 2 * height)):
            w = both_panels(first_core, parts[q][...], rows_of(got_ref, q, height))
            out_ref[at, :] = base_ref[at, :] - product(w, a_ref)

    pl.when(core_is(0))(functools.partial(run, True, own_ref))
    pl.when(core_is(1))(functools.partial(run, False, other_ref))


def final_kernel(count, early, info_ref, a_ref, after_ref, got_ref, *refs):
    first, second = refs[:count], refs[count:2 * count]
    got_early, got_late = refs[2 * count:2 * count + 2]
    coef_ref, resid_ref = refs[2 * count + 2:]
    height = first[0].shape[0]
    places = spans(info_ref, count, 2 * height)

    @pl.when(core_is(0))
    def _():
        for q, at in enumerate(places):
            w = both_panels(True, first[q][...], rows_of(got_ref, q, height))
            coef_ref[at, :] = w.astype(F32)
        resid_ref[...] = after_ref[...]

    @pl.when(core_is(1))
    def _():
        for q, at in enumerate(places):
            source, k = (got_early, q) if q < early else (got_late, q - early)
            w = both_panels(False, second[q][...], rows_of(source, k, height))
            coef_ref[at, :] = w.astype(F32)
            resid_ref[at, :] = after_ref[at, :] - product(w, a_ref)


def base_kernel(count, info_ref, turned_ref, got_ref, *refs):
    parts, out_ref = refs[:count], refs[count]
    height = parts[0].shape[0]
    first_plane = lax.axis_index("grp") < CORES

    @pl.when(first_plane)
    def _():
        out_ref[...] = turned_ref[...]

    def run(first_core):
        for q, at in enumerate(spans(info_ref, count, 2 * height)):
            r = both_panels(first_core, parts[q][...], rows_of(got_ref, q, height))
            out_ref[at, :] = r.astype(F32)

    later = jnp.logical_not(first_plane)
    pl.when(jnp.logical_and(later, core_is(0)))(functools.partial(run, True))
    pl.when(jnp.logical_and(later, core_is(1)))(functools.partial(run, False))


def local_call(body, out_shape, info, arrays):
    many = isinstance(out_shape, (list, tuple))
    return pl.pallas_call(
        body,
        out_shape=out_shape,
        in_specs=[pl.BlockSpec(memory_space=pltpu.SMEM)] + [VMEM] * len(arrays),
        out_specs=[VMEM] * len(out_shape) if many else VMEM,
        compiler_params=pltpu.CompilerParams(vmem_limit_bytes=GRANT),
    )(info, *arrays)


def first_call(owner, layout, panel, own, other):
    feats = own[0].shape[1]
    width, rows = panel.shape
    return pl.pallas_call(
        functools.partial(first_kernel, layout, owner),
        out_shape=jax.ShapeDtypeStruct((width, feats), BF16),
        in_specs=[VMEM] * (1 + 2 * len(own)),
        out_specs=VMEM,
        cost_estimate=pl.CostEstimate(
            flops=2 * width * rows * feats, bytes_accessed=2 * rows * feats, transcendentals=0
        ),
        compiler_params=pltpu.CompilerParams(vmem_limit_bytes=GRANT),
        name="first_corr",
    )(panel, *own, *other)


def stage_call(owner, layout, panel, ca, cb, squares, own, other, kind):
    feats = own[0].shape[1]
    width, rows = panel.shape
    return pl.pallas_call(
        functools.partial(stage_kernel, layout, owner),
        out_shape=[jax.ShapeDtypeStruct((width, feats), BF16), jax.ShapeDtypeStruct(panel.shape, kind)],
        in_specs=[VMEM] * (5 + 2 * len(own)),
        out_specs=[VMEM] * 2,
        cost_estimate=pl.CostEstimate(
            flops=2 * width * feats * (2 * feats + rows),
            bytes_accessed=2 * feats * (feats + rows),
            transcendentals=0,
        ),
        compiler_params=pltpu.CompilerParams(vmem_limit_bytes=GRANT),
        name="sweep_stage",
    )(panel, ca, cb, *squares, *own, *other)


def sweep(features, residual, precond):
    grp_count, row_count = lax.axis_size("grp"), lax.axis_size("row")
    g, r = lax.axis_index("grp"), lax.axis_index("row")
    core = g % CORES
    plane = g // CORES
    plane_count = grp_count // CORES
    rows, feats = features.shape
    targets = residual.shape[1]
    panel_count = row_count // PAIR * CORES
    width = targets // panel_count

    def permute(x, mask=0, flip=0, keep=None, shift=0):
        route = []
        for a in range(grp_count):
            if keep is not None and a % CORES != keep:
                continue
            b = (a ^ flip) + shift
            if b >= grp_count:
                continue
            for i in range(row_count):
                route.append((a * row_count + i, b * row_count + (i ^ mask)))
        return lax.ppermute(x, ("grp", "row"), route)

    bits = [1 << i for i in range(row_count.bit_length() - 1) if (1 << i) != PAIR]
    masks = [0]
    for bit in reversed(bits):
        masks += [m ^ bit for m in masks]

    def place_of(index):
        return (index // (2 * PAIR)) * PAIR + index % PAIR

    def after(x, *others):
        return lax.optimization_barrier((x,) + others)[0]

    ranks = jnp.stack([place_of(r ^ m) for m in masks])

    def ordered(parts):
        if CORES * width % TILE == 0:
            return parts
        stacked = jnp.take(jnp.stack(parts), jnp.argsort(ranks), axis=0)
        return [stacked[q] for q in range(len(parts))]

    info = jnp.stack(
        [place_of(r ^ m) * CORES * width for m in masks]
    ).astype(jnp.int32)
    starts = [((place_of(r ^ m) * CORES + core) * width).astype(jnp.uint32) for m in masks]
    on_first = core == 0
    at_plane = [plane == step for step in range(plane_count)]
    features, info, starts, on_first, at_plane = lax.optimization_barrier(
        (features, info, starts, on_first, at_plane)
    )
    far = bits[-1]
    near = bits[:-1]
    count = len(masks)
    halves = [features[:, : feats // 2], features[:, feats // 2 :]]

    held = {0: [features]}
    held[far] = [permute(x, mask=far) for x in halves]
    for bit in reversed(near):
        for m in masks:
            if m not in held and (m ^ bit) in held and not m & far:
                held[m] = [permute(x, mask=bit) for x in held[m ^ bit]]
    swapped = permute(features, flip=1)
    square = after(precond, swapped).astype(BF16)
    squares = (square, permute(square, flip=1))

    turned = residual.T
    zero = jnp.uint32(0)

    def slice_for(k):
        return lax.dynamic_slice(turned, (starts[k], zero), (width, rows))

    slices = [slice_for(k).astype(BF16) if m else slice_for(k) for k, m in enumerate(masks)]
    moved = [permute(x, mask=m) for x, m in zip(slices, masks) if m]
    panel = jnp.concatenate([slices[0]] + [x.astype(F32) for x in moved], axis=1)

    held[far][0], squares = lax.optimization_barrier((held[far][0], squares))
    for bit in reversed(near):
        for m in masks:
            if m not in held and (m ^ bit) in held and m & far:
                held[m] = [permute(x, mask=bit) for x in held[m ^ bit]]
    got_blocks = {0: [swapped]}
    for m in masks[1:]:
        got_blocks[m] = [permute(x, flip=1) for x in held[m]]
    layout = [len(held[m]) for m in masks]
    mine = [x for m in masks for x in held[m]]
    theirs = [x for m in masks for x in got_blocks[m]]

    keep_first = keep_second = passed = blocks = None
    for step in range(plane_count):
        end = step + 1 == plane_count
        corr = first_call(0, layout, panel, mine, theirs)
        got = permute(corr, mask=PAIR)
        if end and passed is not None:
            blocks = [passed[:, k * rows:(k + 1) * rows] for k in range(count)]
            blocks = [permute(x, mask=m) if m else x for x, m in zip(blocks, masks)]
        w1, panel1 = stage_call(0, layout, panel, corr, got, squares, mine, theirs, F32)
        keep_first = w1 if keep_first is None else jnp.where(at_plane[step], w1, keep_first)
        corr = first_call(1, layout, panel1, mine, theirs)
        got = permute(corr, mask=PAIR)
        w2, panel2 = stage_call(1, layout, panel1, corr, got, squares, mine, theirs, BF16)
        keep_second = w2 if keep_second is None else jnp.where(at_plane[step], w2, keep_second)
        if not end:
            panel = permute(panel2, shift=CORES)
            passed = panel if passed is None else jnp.where(at_plane[step + 1], panel, passed)

    def gather(pair):
        parts = {0: pair}
        for bit in reversed(bits):
            for m in list(parts):
                parts[m ^ bit] = permute(parts[m], mask=bit)
        return ordered([parts[m] for m in masks])

    first_parts = gather(keep_first)
    second_parts = gather(keep_second)
    first_got = permute(jnp.concatenate(first_parts, axis=0), flip=1)
    early = max(count - 1, 1)
    got_early = permute(jnp.concatenate(second_parts[:early], axis=0), flip=1)
    whole = jax.ShapeDtypeStruct((targets, rows), F32)
    base = turned
    if blocks is not None:
        blocks = ordered(blocks)
        base_got = permute(jnp.concatenate(blocks, axis=0), flip=1)
        base = local_call(
            functools.partial(base_kernel, count), whole, info, [turned, base_got] + blocks
        )
    after_first = local_call(
        functools.partial(update_kernel, count),
        whole,
        info,
        [features, swapped, base, first_got] + first_parts,
    )
    late = second_parts[early:] or second_parts[:1]
    got_late = permute(after(jnp.concatenate(late, axis=0), after_first), flip=1)
    coef_t, resid_t = local_call(
        functools.partial(final_kernel, count, early),
        [jax.ShapeDtypeStruct((targets, feats), F32), whole],
        info,
        [features, after_first, first_got] + first_parts + second_parts + [got_early, got_late],
    )
    return coef_t.T, resid_t.T[None]


def solution(mesh):
    placed = (P("row", "grp"), P("row", None), P("grp", None))

    return jax.shard_map(
        sweep,
        mesh=mesh,
        in_specs=placed,
        out_specs=(P("grp", None), P("grp", "row", None)),
        check_vma=False,
    )
```

```python
import functools

import jax
import jax.numpy as jnp
from jax import lax
from jax.experimental import pallas as pl
from jax.experimental.pallas import tpu as pltpu
from jax.sharding import PartitionSpec as P


F32 = jnp.float32
BF16 = jnp.bfloat16
CORES = 2
PAIR = 2
TILE = 8
ANY = pl.BlockSpec(memory_space=pl.ANY)
VMEM = pl.BlockSpec(memory_space=pltpu.VMEM)
GRANT = 24 * 1024 * 1024


def grouped(refs, layout):
    out, at = [], 0
    for size in layout:
        out.append(refs[at:at + size])
        at += size
    return out


def correlation(r_ref, blocks, c_ref):
    rows, feats = blocks[0][0].shape[0], c_ref.shape[1]
    cut = feats // 2
    whole = [(q, b[0]) for q, b in enumerate(blocks) if len(b) == 1]
    split = [(q, b) for q, b in enumerate(blocks) if len(b) == 2]
    lhs = [r_ref[:, q * rows:(q + 1) * rows].astype(BF16) for q in range(len(blocks))]
    for k in range(2):
        span = pl.ds(k * cut, cut)
        total = None
        for q, block in whole:
            part = jnp.dot(lhs[q], block[:, span], preferred_element_type=F32)
            total = part if total is None else total + part
        for q, block in split:
            total += jnp.dot(lhs[q], block[k][...], preferred_element_type=F32)
        c_ref[:, span] = total.astype(BF16)


def core_is(index):
    return lax.axis_index("grp") % CORES == index


def first_kernel(layout, owner, r_ref, *refs):
    count = sum(layout)

    @pl.when(core_is(owner))
    def _():
        correlation(r_ref, grouped(refs[:count], layout), refs[2 * count])

    @pl.when(core_is(1 - owner))
    def _():
        correlation(r_ref, grouped(refs[count:2 * count], layout), refs[2 * count])


def stage_kernel(layout, owner, r_ref, ca_ref, cb_ref, own_ref, other_ref, *refs):
    count = sum(layout)
    w_ref, rn_ref = refs[2 * count], refs[2 * count + 1:]
    width = ca_ref.shape[0]
    total = ca_ref[...].astype(F32) + cb_ref[...].astype(F32)
    high = total.astype(BF16)
    low = (total - high.astype(F32)).astype(BF16)
    stacked = jnp.concatenate((high, low), axis=0)

    def run(map_ref, blocks):
        both = jnp.dot(stacked, map_ref[...], preferred_element_type=F32)
        wb = (both[:width] + both[width:]).astype(BF16)
        w_ref[...] = wb
        if not rn_ref:
            return
        rows = blocks[0][0].shape[0]
        cut = wb.shape[1] // 2
        for q, block in enumerate(blocks):
            span = pl.ds(q * rows, rows)
            if len(block) == 1:
                change = product(wb, block[0])
            else:
                change = product(wb[:, :cut], block[0]) + product(wb[:, cut:], block[1])
            rn_ref[0][:, span] = (r_ref[:, span].astype(F32) - change).astype(rn_ref[0].dtype)

    @pl.when(core_is(owner))
    def _():
        run(own_ref, grouped(refs[:count], layout))

    @pl.when(core_is(1 - owner))
    def _():
        run(other_ref, grouped(refs[count:2 * count], layout))


def product(w, a_ref):
    return lax.dot_general(w, a_ref[...], (((1,), (1,)), ((), ())), preferred_element_type=F32)


def place_of(index):
    return (index // (2 * PAIR)) * PAIR + index % PAIR


def spans(masks, height):
    if height % TILE:
        return [pl.ds(q * height, height) for q in range(len(masks))]
    shard = lax.axis_index("row")
    places = [place_of(lax.bitwise_xor(shard, jnp.int32(m))) for m in masks]
    return [pl.ds(pl.multiple_of(place * height, TILE), height) for place in places]


def rows_of(ref, q, height):
    return ref[q * height:(q + 1) * height, :]


def both_panels(first_core, own, got):
    return jnp.concatenate((own, got) if first_core else (got, own), axis=0)


def update_kernel(masks, own_ref, other_ref, base_ref, got_ref, *refs):
    parts, out_ref = refs[:-1], refs[-1]
    height = parts[0].shape[0]

    def run(first_core, a_ref):
        for q, at in enumerate(spans(masks, 2 * height)):
            w = both_panels(first_core, parts[q][...], rows_of(got_ref, q, height))
            out_ref[at, :] = base_ref[at, :] - product(w, a_ref)

    pl.when(core_is(0))(functools.partial(run, True, own_ref))
    pl.when(core_is(1))(functools.partial(run, False, other_ref))


def write_kernel(masks, chosen, resume, a_ref, after_ref, got_ref, got_late_ref, *refs):
    count = len(masks)
    first, second = refs[:count], refs[count:2 * count]
    refs = refs[2 * count + (2 if resume else 0):]
    coef_ref, resid_ref, coefs, resids, sems = refs
    height = first[0].shape[0]
    places = spans(masks, 2 * height)

    def copies(k):
        at = places[chosen[k]]
        return (
            pltpu.make_async_copy(coefs.at[k], coef_ref.at[at, :], sems.at[0, k]),
            pltpu.make_async_copy(resids.at[k], resid_ref.at[at, :], sems.at[1, k]),
        )

    for k, q in enumerate(chosen):
        @pl.when(core_is(0))
        def _():
            w = both_panels(True, first[q][...], rows_of(got_ref, q, height))
            coefs[k] = w.astype(F32)
            resids[k] = after_ref[places[q], :]

        @pl.when(core_is(1))
        def _():
            w = both_panels(False, second[q][...], rows_of(got_late_ref, k, height))
            coefs[k] = w.astype(F32)
            resids[k] = after_ref[places[q], :] - product(w, a_ref)

        for copy in copies(k):
            copy.start()
    for k in range(len(chosen)):
        for copy in copies(k):
            copy.wait()


def write_call(masks, chosen, shapes, arrays, resume=()):
    height = 2 * arrays[4].shape[0]
    feats, rows = shapes[0].shape[1], shapes[1].shape[1]
    size = len(chosen)
    return pl.pallas_call(
        functools.partial(write_kernel, masks, chosen, len(resume) > 0),
        out_shape=shapes,
        in_specs=[VMEM] * len(arrays) + [ANY] * len(resume),
        out_specs=[ANY] * 2,
        scratch_shapes=[
            pltpu.VMEM((size, height, feats), F32),
            pltpu.VMEM((size, height, rows), F32),
            pltpu.SemaphoreType.DMA((2, size)),
        ],
        input_output_aliases={len(arrays) + k: k for k in range(len(resume))},
        compiler_params=pltpu.CompilerParams(vmem_limit_bytes=GRANT),
        name="write_rest" if resume else "write_early",
    )(*arrays, *resume)


def base_kernel(masks, turned_ref, got_ref, *refs):
    parts, out_ref = refs[:-1], refs[-1]
    height = parts[0].shape[0]
    first_plane = lax.axis_index("grp") < CORES

    @pl.when(first_plane)
    def _():
        out_ref[...] = turned_ref[...]

    def run(first_core):
        for q, at in enumerate(spans(masks, 2 * height)):
            r = both_panels(first_core, parts[q][...], rows_of(got_ref, q, height))
            out_ref[at, :] = r.astype(F32)

    later = jnp.logical_not(first_plane)
    pl.when(jnp.logical_and(later, core_is(0)))(functools.partial(run, True))
    pl.when(jnp.logical_and(later, core_is(1)))(functools.partial(run, False))


def local_call(body, out_shape, arrays):
    many = isinstance(out_shape, (list, tuple))
    return pl.pallas_call(
        body,
        out_shape=out_shape,
        in_specs=[VMEM] * len(arrays),
        out_specs=[VMEM] * len(out_shape) if many else VMEM,
        compiler_params=pltpu.CompilerParams(vmem_limit_bytes=GRANT),
    )(*arrays)


def first_call(owner, layout, panel, own, other):
    feats = own[0].shape[1]
    width, rows = panel.shape
    return pl.pallas_call(
        functools.partial(first_kernel, layout, owner),
        out_shape=jax.ShapeDtypeStruct((width, feats), BF16),
        in_specs=[VMEM] * (1 + 2 * len(own)),
        out_specs=VMEM,
        cost_estimate=pl.CostEstimate(
            flops=2 * width * rows * feats, bytes_accessed=2 * rows * feats, transcendentals=0
        ),
        compiler_params=pltpu.CompilerParams(vmem_limit_bytes=GRANT),
        name="first_corr",
    )(panel, *own, *other)


def stage_call(owner, layout, panel, ca, cb, squares, own, other, kind):
    feats = own[0].shape[1]
    width, rows = panel.shape
    out_shape = [jax.ShapeDtypeStruct((width, feats), BF16)]
    if kind is None:
        own, other, layout = [panel], [panel], [1]
    else:
        out_shape.append(jax.ShapeDtypeStruct(panel.shape, kind))
    return pl.pallas_call(
        functools.partial(stage_kernel, layout, owner),
        out_shape=out_shape,
        in_specs=[VMEM] * (5 + 2 * len(own)),
        out_specs=[VMEM] * len(out_shape),
        cost_estimate=pl.CostEstimate(
            flops=2 * width * feats * (2 * feats + rows),
            bytes_accessed=2 * feats * (feats + rows),
            transcendentals=0,
        ),
        compiler_params=pltpu.CompilerParams(vmem_limit_bytes=GRANT),
        name="sweep_stage",
    )(panel, ca, cb, *squares, *own, *other)


def sweep(features, residual, precond):
    grp_count, row_count = lax.axis_size("grp"), lax.axis_size("row")
    g, r = lax.axis_index("grp"), lax.axis_index("row")
    core = g % CORES
    plane = g // CORES
    plane_count = grp_count // CORES
    rows, feats = features.shape
    targets = residual.shape[1]
    panel_count = row_count // PAIR * CORES
    width = targets // panel_count

    def permute(x, mask=0, flip=0, keep=None, shift=0):
        route = []
        for a in range(grp_count):
            if keep is not None and a % CORES != keep:
                continue
            b = (a ^ flip) + shift
            if b >= grp_count:
                continue
            for i in range(row_count):
                route.append((a * row_count + i, b * row_count + (i ^ mask)))
        return lax.ppermute(x, ("grp", "row"), route)

    bits = [1 << i for i in range(row_count.bit_length() - 1) if (1 << i) != PAIR]
    masks = [0]
    for bit in reversed(bits):
        masks += [m ^ bit for m in masks]

    def after(x, *others):
        return lax.optimization_barrier((x,) + others)[0]

    ranks = jnp.stack([place_of(r ^ m) for m in masks])

    def ordered(parts):
        if CORES * width % TILE == 0:
            return parts
        stacked = jnp.take(jnp.stack(parts), jnp.argsort(ranks), axis=0)
        return [stacked[q] for q in range(len(parts))]

    starts = [((place_of(r ^ m) * CORES + core) * width).astype(jnp.uint32) for m in masks]
    on_first = core == 0
    at_plane = [plane == step for step in range(plane_count)]
    features, starts, on_first, at_plane = lax.optimization_barrier(
        (features, starts, on_first, at_plane)
    )
    far = bits[-1]
    near = bits[:-1]
    count = len(masks)
    halves = [features[:, : feats // 2], features[:, feats // 2 :]]

    held = {0: [features]}
    held[far] = [permute(x, mask=far) for x in halves]
    for bit in reversed(near):
        for m in masks:
            if m not in held and (m ^ bit) in held and not m & far:
                held[m] = [permute(x, mask=bit) for x in held[m ^ bit]]
    swapped = permute(features, flip=1)
    square = after(precond, swapped).astype(BF16)
    squares = (square, permute(square, flip=1))

    turned = residual.T
    zero = jnp.uint32(0)

    def slice_for(k):
        return lax.dynamic_slice(turned, (starts[k], zero), (width, rows))

    slices = [slice_for(k).astype(BF16) if m else slice_for(k) for k, m in enumerate(masks)]
    moved = [permute(x, mask=m) for x, m in zip(slices, masks) if m]
    panel = jnp.concatenate([slices[0]] + [x.astype(F32) for x in moved], axis=1)

    held[far][0], squares = lax.optimization_barrier((held[far][0], squares))
    for bit in reversed(near):
        for m in masks:
            if m not in held and (m ^ bit) in held and m & far:
                held[m] = [permute(x, mask=bit) for x in held[m ^ bit]]
    got_blocks = {0: [swapped]}
    for m in masks[1:]:
        got_blocks[m] = [permute(x, flip=1) for x in held[m]]
    layout = [len(held[m]) for m in masks]
    mine = [x for m in masks for x in held[m]]
    theirs = [x for m in masks for x in got_blocks[m]]

    keep_first = keep_second = passed = blocks = None
    for step in range(plane_count):
        end = step + 1 == plane_count
        corr = first_call(0, layout, panel, mine, theirs)
        got = permute(corr, mask=PAIR)
        if end and passed is not None:
            blocks = [passed[:, k * rows:(k + 1) * rows] for k in range(count)]
            blocks = [permute(x, mask=m) if m else x for x, m in zip(blocks, masks)]
        w1, panel1 = stage_call(0, layout, panel, corr, got, squares, mine, theirs, F32)
        keep_first = w1 if keep_first is None else jnp.where(at_plane[step], w1, keep_first)
        corr = first_call(1, layout, panel1, mine, theirs)
        got = permute(corr, mask=PAIR)
        w2, *panel2 = stage_call(
            1, layout, panel1, corr, got, squares, mine, theirs, None if end else BF16
        )
        keep_second = w2 if keep_second is None else jnp.where(at_plane[step], w2, keep_second)
        if not end:
            panel = permute(panel2[0], shift=CORES)
            passed = panel if passed is None else jnp.where(at_plane[step + 1], panel, passed)

    def gather(pair):
        parts = {0: pair}
        for bit in reversed(bits):
            for m in list(parts):
                parts[m ^ bit] = permute(parts[m], mask=bit)
        return ordered([parts[m] for m in masks])

    first_parts = gather(keep_first)
    second_parts = gather(keep_second)
    first_got = permute(jnp.concatenate(first_parts, axis=0), flip=1)
    early = max(count - 1, 1)
    got_early = permute(jnp.concatenate(second_parts[:early], axis=0), flip=1)
    whole = jax.ShapeDtypeStruct((targets, rows), F32)
    base = turned
    if blocks is not None:
        blocks = ordered(blocks)
        base_got = permute(jnp.concatenate(blocks, axis=0), flip=1)
        base = local_call(functools.partial(base_kernel, masks), whole, [turned, base_got] + blocks)
    after_first = local_call(
        functools.partial(update_kernel, masks),
        whole,
        [features, swapped, base, first_got] + first_parts,
    )
    if CORES * width % TILE:
        def assembled(parts, got):
            got = [got[q * width:(q + 1) * width] for q in range(len(parts))]
            pairs = [
                jnp.where(on_first, jnp.concatenate((x, y), axis=0), jnp.concatenate((y, x), axis=0))
                for x, y in zip(parts, got)
            ]
            return jnp.concatenate(pairs, axis=0)

        got_all = [got_early]
        if early < count:
            late = jnp.concatenate(second_parts[early:], axis=0)
            got_all.append(permute(late, flip=1))
        second = assembled(second_parts, jnp.concatenate(got_all, axis=0))
        coef_t = jnp.where(on_first, assembled(first_parts, first_got), second).astype(F32)
        change = product(second, features)
        return coef_t.T, jnp.where(on_first, after_first, after_first - change).T[None]
    shapes = [jax.ShapeDtypeStruct((targets, feats), F32), whole]
    parts = [features, after_first, first_got]
    known = second_parts[:early] + second_parts[:1] * (count - early)
    done = write_call(masks, tuple(range(early)), shapes, parts + [got_early] + first_parts + known)
    if early < count:
        late = jnp.concatenate(second_parts[early:], axis=0)
        got_late = permute(late, flip=1)
        done = write_call(
            masks,
            tuple(range(early, count)),
            shapes,
            parts + [got_late] + first_parts + second_parts,
            done,
        )
    coef_t, resid_t = done
    return coef_t.T, resid_t.T[None]


def solution(mesh):
    placed = (P("row", "grp"), P("row", None), P("grp", None))

    return jax.shard_map(
        sweep,
        mesh=mesh,
        in_specs=placed,
        out_specs=(P("grp", None), P("grp", "row", None)),
        check_vma=False,
    )
```

```python
import functools

import jax
import jax.numpy as jnp
from jax import lax
from jax.experimental import pallas as pl
from jax.experimental.pallas import tpu as pltpu
from jax.sharding import PartitionSpec as P


F32 = jnp.float32
BF16 = jnp.bfloat16
CORES = 2
PAIR = 2
CUTS = (0, 2, 4, 6, 8)
TILE = 8
ANY = pl.BlockSpec(memory_space=pl.ANY)
VMEM = pl.BlockSpec(memory_space=pltpu.VMEM)
GRANT = 24 * 1024 * 1024


def grouped(refs, layout):
    out, at = [], 0
    for size in layout:
        out.append(refs[at:at + size])
        at += size
    return out


def correlation(r_ref, blocks, c_ref):
    rows = blocks[0][0].shape[0]
    split = max(blocks, key=len)
    lhs = [r_ref[:, q * rows:(q + 1) * rows].astype(BF16) for q in range(len(blocks))]
    start = 0
    for k, piece in enumerate(split):
        span = pl.ds(start, piece.shape[1])
        total = None
        for x, block in zip(lhs, blocks):
            part = block[0][:, span] if len(block) == 1 else block[k][...]
            part = jnp.dot(x, part, preferred_element_type=F32)
            total = part if total is None else total + part
        c_ref[:, span] = total.astype(BF16)
        start += piece.shape[1]


def core_is(index):
    return lax.axis_index("grp") % CORES == index


def first_kernel(layout, owner, r_ref, *refs):
    count = sum(layout)

    @pl.when(core_is(owner))
    def _():
        correlation(r_ref, grouped(refs[:count], layout), refs[2 * count])

    @pl.when(core_is(1 - owner))
    def _():
        correlation(r_ref, grouped(refs[count:2 * count], layout), refs[2 * count])


def stage_kernel(layout, owner, r_ref, ca_ref, cb_ref, own_ref, other_ref, *refs):
    count = sum(layout)
    w_ref, rn_ref = refs[2 * count], refs[2 * count + 1:]
    width = ca_ref.shape[0]
    total = ca_ref[...].astype(F32) + cb_ref[...].astype(F32)
    high = total.astype(BF16)
    low = (total - high.astype(F32)).astype(BF16)
    stacked = jnp.concatenate((high, low), axis=0)

    def run(map_ref, blocks):
        both = jnp.dot(stacked, map_ref[...], preferred_element_type=F32)
        wb = (both[:width] + both[width:]).astype(BF16)
        w_ref[...] = wb
        if not rn_ref:
            return
        rows = blocks[0][0].shape[0]
        for q, block in enumerate(blocks):
            span = pl.ds(q * rows, rows)
            change, start = None, 0
            for piece in block:
                size = piece.shape[1]
                part = product(wb[:, start:start + size], piece)
                change = part if change is None else change + part
                start += size
            rn_ref[0][:, span] = (r_ref[:, span].astype(F32) - change).astype(rn_ref[0].dtype)

    @pl.when(core_is(owner))
    def _():
        run(own_ref, grouped(refs[:count], layout))

    @pl.when(core_is(1 - owner))
    def _():
        run(other_ref, grouped(refs[count:2 * count], layout))


def product(w, a_ref):
    return lax.dot_general(w, a_ref[...], (((1,), (1,)), ((), ())), preferred_element_type=F32)


def place_of(index):
    return (index // (2 * PAIR)) * PAIR + index % PAIR


def spans(masks, height):
    if height % TILE:
        return [pl.ds(q * height, height) for q in range(len(masks))]
    shard = lax.axis_index("row")
    places = [place_of(lax.bitwise_xor(shard, jnp.int32(m))) for m in masks]
    return [pl.ds(pl.multiple_of(place * height, TILE), height) for place in places]


def rows_of(ref, q, height):
    return ref[q * height:(q + 1) * height, :]


def both_panels(first_core, own, got):
    return jnp.concatenate((own, got) if first_core else (got, own), axis=0)


def update_kernel(masks, own_ref, other_ref, base_ref, got_ref, *refs):
    parts, out_ref = refs[:-1], refs[-1]
    height = parts[0].shape[0]

    def run(first_core, a_ref):
        for q, at in enumerate(spans(masks, 2 * height)):
            w = both_panels(first_core, parts[q][...], rows_of(got_ref, q, height))
            out_ref[at, :] = base_ref[at, :] - product(w, a_ref)

    pl.when(core_is(0))(functools.partial(run, True, own_ref))
    pl.when(core_is(1))(functools.partial(run, False, other_ref))


def write_kernel(masks, chosen, resume, a_ref, after_ref, got_ref, got_late_ref, *refs):
    count = len(masks)
    first, second = refs[:count], refs[count:2 * count]
    refs = refs[2 * count + (2 if resume else 0):]
    coef_ref, resid_ref, coefs, resids, sems = refs
    height = first[0].shape[0]
    places = spans(masks, 2 * height)

    def copies(k):
        at = places[chosen[k]]
        return (
            pltpu.make_async_copy(coefs.at[k], coef_ref.at[at, :], sems.at[0, k]),
            pltpu.make_async_copy(resids.at[k], resid_ref.at[at, :], sems.at[1, k]),
        )

    for k, q in enumerate(chosen):
        @pl.when(core_is(0))
        def _():
            w = both_panels(True, first[q][...], rows_of(got_ref, q, height))
            coefs[k] = w.astype(F32)
            resids[k] = after_ref[places[q], :]

        @pl.when(core_is(1))
        def _():
            w = both_panels(False, second[q][...], rows_of(got_late_ref, k, height))
            coefs[k] = w.astype(F32)
            resids[k] = after_ref[places[q], :] - product(w, a_ref)

        for copy in copies(k):
            copy.start()
    for k in range(len(chosen)):
        for copy in copies(k):
            copy.wait()


def write_call(masks, chosen, shapes, arrays, resume=()):
    height = 2 * arrays[4].shape[0]
    feats, rows = shapes[0].shape[1], shapes[1].shape[1]
    size = len(chosen)
    return pl.pallas_call(
        functools.partial(write_kernel, masks, chosen, len(resume) > 0),
        out_shape=shapes,
        in_specs=[VMEM] * len(arrays) + [ANY] * len(resume),
        out_specs=[ANY] * 2,
        scratch_shapes=[
            pltpu.VMEM((size, height, feats), F32),
            pltpu.VMEM((size, height, rows), F32),
            pltpu.SemaphoreType.DMA((2, size)),
        ],
        input_output_aliases={len(arrays) + k: k for k in range(len(resume))},
        compiler_params=pltpu.CompilerParams(vmem_limit_bytes=GRANT),
        name="write_rest" if resume else "write_early",
    )(*arrays, *resume)


def base_kernel(masks, turned_ref, got_ref, *refs):
    parts, out_ref = refs[:-1], refs[-1]
    height = parts[0].shape[0]
    first_plane = lax.axis_index("grp") < CORES

    @pl.when(first_plane)
    def _():
        out_ref[...] = turned_ref[...]

    def run(first_core):
        for q, at in enumerate(spans(masks, 2 * height)):
            r = both_panels(first_core, parts[q][...], rows_of(got_ref, q, height))
            out_ref[at, :] = r.astype(F32)

    later = jnp.logical_not(first_plane)
    pl.when(jnp.logical_and(later, core_is(0)))(functools.partial(run, True))
    pl.when(jnp.logical_and(later, core_is(1)))(functools.partial(run, False))


def local_call(body, out_shape, arrays):
    many = isinstance(out_shape, (list, tuple))
    return pl.pallas_call(
        body,
        out_shape=out_shape,
        in_specs=[VMEM] * len(arrays),
        out_specs=[VMEM] * len(out_shape) if many else VMEM,
        compiler_params=pltpu.CompilerParams(vmem_limit_bytes=GRANT),
    )(*arrays)


def first_call(owner, layout, panel, own, other):
    feats = own[0].shape[1]
    width, rows = panel.shape
    return pl.pallas_call(
        functools.partial(first_kernel, layout, owner),
        out_shape=jax.ShapeDtypeStruct((width, feats), BF16),
        in_specs=[VMEM] * (1 + 2 * len(own)),
        out_specs=VMEM,
        cost_estimate=pl.CostEstimate(
            flops=2 * width * rows * feats, bytes_accessed=2 * rows * feats, transcendentals=0
        ),
        compiler_params=pltpu.CompilerParams(vmem_limit_bytes=GRANT),
        name="first_corr",
    )(panel, *own, *other)


def stage_call(owner, layout, panel, ca, cb, squares, own, other, kind):
    feats = own[0].shape[1]
    width, rows = panel.shape
    out_shape = [jax.ShapeDtypeStruct((width, feats), BF16)]
    if kind is None:
        own, other, layout = [panel], [panel], [1]
    else:
        out_shape.append(jax.ShapeDtypeStruct(panel.shape, kind))
    return pl.pallas_call(
        functools.partial(stage_kernel, layout, owner),
        out_shape=out_shape,
        in_specs=[VMEM] * (5 + 2 * len(own)),
        out_specs=[VMEM] * len(out_shape),
        cost_estimate=pl.CostEstimate(
            flops=2 * width * feats * (2 * feats + rows),
            bytes_accessed=2 * feats * (feats + rows),
            transcendentals=0,
        ),
        compiler_params=pltpu.CompilerParams(vmem_limit_bytes=GRANT),
        name="sweep_stage",
    )(panel, ca, cb, *squares, *own, *other)


def sweep(features, residual, precond):
    grp_count, row_count = lax.axis_size("grp"), lax.axis_size("row")
    g, r = lax.axis_index("grp"), lax.axis_index("row")
    core = g % CORES
    plane = g // CORES
    plane_count = grp_count // CORES
    rows, feats = features.shape
    targets = residual.shape[1]
    panel_count = row_count // PAIR * CORES
    width = targets // panel_count

    def permute(x, mask=0, flip=0, keep=None, shift=0):
        route = []
        for a in range(grp_count):
            if keep is not None and a % CORES != keep:
                continue
            b = (a ^ flip) + shift
            if b >= grp_count:
                continue
            for i in range(row_count):
                route.append((a * row_count + i, b * row_count + (i ^ mask)))
        return lax.ppermute(x, ("grp", "row"), route)

    bits = [1 << i for i in range(row_count.bit_length() - 1) if (1 << i) != PAIR]
    masks = [0]
    for bit in reversed(bits):
        masks += [m ^ bit for m in masks]

    def after(x, *others):
        return lax.optimization_barrier((x,) + others)[0]

    ranks = jnp.stack([place_of(r ^ m) for m in masks])

    def ordered(parts):
        if CORES * width % TILE == 0:
            return parts
        stacked = jnp.take(jnp.stack(parts), jnp.argsort(ranks), axis=0)
        return [stacked[q] for q in range(len(parts))]

    starts = [((place_of(r ^ m) * CORES + core) * width).astype(jnp.uint32) for m in masks]
    on_first = core == 0
    at_plane = [plane == step for step in range(plane_count)]
    features, starts, on_first, at_plane = lax.optimization_barrier(
        (features, starts, on_first, at_plane)
    )
    far = bits[-1]
    near = bits[:-1]
    count = len(masks)
    edges = [feats * e // CUTS[-1] for e in CUTS]
    parts_of_a = [features[:, low:high] for low, high in zip(edges[:-1], edges[1:])]

    held = {0: [features]}
    held[far] = [permute(x, mask=far) for x in parts_of_a]
    for bit in reversed(near):
        for m in masks:
            if m not in held and (m ^ bit) in held and not m & far:
                held[m] = [permute(x, mask=bit) for x in held[m ^ bit]]
    swapped = permute(features, flip=1)
    square = after(precond, swapped).astype(BF16)
    squares = (square, permute(square, flip=1))

    turned = residual.T
    zero = jnp.uint32(0)

    def slice_for(k):
        return lax.dynamic_slice(turned, (starts[k], zero), (width, rows))

    slices = [slice_for(k).astype(BF16) if m else slice_for(k) for k, m in enumerate(masks)]
    moved = [permute(x, mask=m) for x, m in zip(slices, masks) if m]
    panel = jnp.concatenate([slices[0]] + [x.astype(F32) for x in moved], axis=1)

    held[far][0], squares = lax.optimization_barrier((held[far][0], squares))
    for bit in reversed(near):
        for m in masks:
            if m not in held and (m ^ bit) in held and m & far:
                held[m] = [permute(x, mask=bit) for x in held[m ^ bit]]
    got_blocks = {0: [swapped]}
    for m in masks[1:]:
        got_blocks[m] = [permute(x, flip=1) for x in held[m]]
    layout = [len(held[m]) for m in masks]
    mine = [x for m in masks for x in held[m]]
    theirs = [x for m in masks for x in got_blocks[m]]

    keep_first = keep_second = passed = blocks = None
    for step in range(plane_count):
        end = step + 1 == plane_count
        corr = first_call(0, layout, panel, mine, theirs)
        got = permute(corr, mask=PAIR)
        if end and passed is not None:
            blocks = [passed[:, k * rows:(k + 1) * rows] for k in range(count)]
            blocks = [permute(x, mask=m) if m else x for x, m in zip(blocks, masks)]
        w1, panel1 = stage_call(0, layout, panel, corr, got, squares, mine, theirs, F32)
        keep_first = w1 if keep_first is None else jnp.where(at_plane[step], w1, keep_first)
        corr = first_call(1, layout, panel1, mine, theirs)
        got = permute(corr, mask=PAIR)
        w2, *panel2 = stage_call(
            1, layout, panel1, corr, got, squares, mine, theirs, None if end else BF16
        )
        keep_second = w2 if keep_second is None else jnp.where(at_plane[step], w2, keep_second)
        if not end:
            panel = permute(panel2[0], shift=CORES)
            passed = panel if passed is None else jnp.where(at_plane[step + 1], panel, passed)

    def gather(pair):
        parts = {0: pair}
        for bit in reversed(bits):
            for m in list(parts):
                parts[m ^ bit] = permute(parts[m], mask=bit)
        return ordered([parts[m] for m in masks])

    first_parts = gather(keep_first)
    second_parts = gather(keep_second)
    first_got = permute(jnp.concatenate(first_parts, axis=0), flip=1)
    early = max(count - 1, 1)
    got_early = permute(jnp.concatenate(second_parts[:early], axis=0), flip=1)
    whole = jax.ShapeDtypeStruct((targets, rows), F32)
    base = turned
    if blocks is not None:
        blocks = ordered(blocks)
        base_got = permute(jnp.concatenate(blocks, axis=0), flip=1)
        base = local_call(functools.partial(base_kernel, masks), whole, [turned, base_got] + blocks)
    after_first = local_call(
        functools.partial(update_kernel, masks),
        whole,
        [features, swapped, base, first_got] + first_parts,
    )
    if CORES * width % TILE:
        def assembled(parts, got):
            got = [got[q * width:(q + 1) * width] for q in range(len(parts))]
            pairs = [
                jnp.where(on_first, jnp.concatenate((x, y), axis=0), jnp.concatenate((y, x), axis=0))
                for x, y in zip(parts, got)
            ]
            return jnp.concatenate(pairs, axis=0)

        got_all = [got_early]
        if early < count:
            late = jnp.concatenate(second_parts[early:], axis=0)
            got_all.append(permute(late, flip=1))
        second = assembled(second_parts, jnp.concatenate(got_all, axis=0))
        coef_t = jnp.where(on_first, assembled(first_parts, first_got), second).astype(F32)
        change = product(second, features)
        return coef_t.T, jnp.where(on_first, after_first, after_first - change).T[None]
    shapes = [jax.ShapeDtypeStruct((targets, feats), F32), whole]
    parts = [features, after_first, first_got]
    known = second_parts[:early] + second_parts[:1] * (count - early)
    done = write_call(masks, tuple(range(early)), shapes, parts + [got_early] + first_parts + known)
    if early < count:
        late = jnp.concatenate(second_parts[early:], axis=0)
        got_late = permute(late, flip=1)
        done = write_call(
            masks,
            tuple(range(early, count)),
            shapes,
            parts + [got_late] + first_parts + second_parts,
            done,
        )
    coef_t, resid_t = done
    return coef_t.T, resid_t.T[None]


def solution(mesh):
    placed = (P("row", "grp"), P("row", None), P("grp", None))

    return jax.shard_map(
        sweep,
        mesh=mesh,
        in_specs=placed,
        out_specs=(P("grp", None), P("grp", "row", None)),
        check_vma=False,
    )
```

```python
import functools

import jax
import jax.numpy as jnp
from jax import lax
from jax.experimental import pallas as pl
from jax.experimental.pallas import tpu as pltpu
from jax.sharding import PartitionSpec as P


F32 = jnp.float32
BF16 = jnp.bfloat16
CORES = 2
PAIR = 2
FIRST_PIECES, LAST_PIECES = 1, 2
CUTS = (0, 2, 4, 6, 8)
TILE = 8
ANY = pl.BlockSpec(memory_space=pl.ANY)
VMEM = pl.BlockSpec(memory_space=pltpu.VMEM)
GRANT = 24 * 1024 * 1024


def grouped(refs, layout):
    out, at = [], 0
    for size in layout:
        out.append(refs[at:at + size])
        at += size
    return out


def correlation(r_ref, blocks, c_ref):
    rows = blocks[0][0].shape[0]
    split = max(blocks, key=len)
    lhs = [r_ref[:, q * rows:(q + 1) * rows].astype(BF16) for q in range(len(blocks))]
    start = 0
    for k, piece in enumerate(split):
        span = pl.ds(start, piece.shape[1])
        total = None
        for x, block in zip(lhs, blocks):
            part = block[0][:, span] if len(block) == 1 else block[k][...]
            part = jnp.dot(x, part, preferred_element_type=F32)
            total = part if total is None else total + part
        c_ref[:, span] = total.astype(BF16)
        start += piece.shape[1]


def core_is(index):
    return lax.axis_index("grp") % CORES == index


def first_kernel(layout, owner, r_ref, *refs):
    count = sum(layout)

    @pl.when(core_is(owner))
    def _():
        correlation(r_ref, grouped(refs[:count], layout), refs[2 * count])

    @pl.when(core_is(1 - owner))
    def _():
        correlation(r_ref, grouped(refs[count:2 * count], layout), refs[2 * count])


def stage_kernel(layout, owner, r_ref, ca_ref, cb_ref, own_ref, other_ref, *refs):
    count = sum(layout)
    w_ref, rn_ref = refs[2 * count], refs[2 * count + 1:]
    width = ca_ref.shape[0]
    total = ca_ref[...].astype(F32) + cb_ref[...].astype(F32)
    high = total.astype(BF16)
    low = (total - high.astype(F32)).astype(BF16)
    stacked = jnp.concatenate((high, low), axis=0)

    def run(map_ref, blocks):
        both = jnp.dot(stacked, map_ref[...], preferred_element_type=F32)
        wb = (both[:width] + both[width:]).astype(BF16)
        w_ref[...] = wb
        if not rn_ref:
            return
        rows = blocks[0][0].shape[0]
        for q, block in enumerate(blocks):
            span = pl.ds(q * rows, rows)
            change, start = None, 0
            for piece in block:
                size = piece.shape[1]
                part = product(wb[:, start:start + size], piece)
                change = part if change is None else change + part
                start += size
            rn_ref[0][:, span] = (r_ref[:, span].astype(F32) - change).astype(rn_ref[0].dtype)

    @pl.when(core_is(owner))
    def _():
        run(own_ref, grouped(refs[:count], layout))

    @pl.when(core_is(1 - owner))
    def _():
        run(other_ref, grouped(refs[count:2 * count], layout))


def product(w, a_ref):
    return lax.dot_general(w, a_ref[...], (((1,), (1,)), ((), ())), preferred_element_type=F32)


def place_of(index):
    return (index // (2 * PAIR)) * PAIR + index % PAIR


def spans(masks, height):
    if height % TILE:
        return [pl.ds(q * height, height) for q in range(len(masks))]
    shard = lax.axis_index("row")
    places = [place_of(lax.bitwise_xor(shard, jnp.int32(m))) for m in masks]
    return [pl.ds(pl.multiple_of(place * height, TILE), height) for place in places]


def rows_of(ref, q, height):
    return ref[q * height:(q + 1) * height, :]


def both_panels(first_core, own, got):
    return jnp.concatenate((own, got) if first_core else (got, own), axis=0)


def update_kernel(masks, own_ref, other_ref, base_ref, got_ref, *refs):
    parts, out_ref = refs[:-1], refs[-1]
    height = parts[0].shape[0]

    def run(first_core, a_ref):
        for q, at in enumerate(spans(masks, 2 * height)):
            w = both_panels(first_core, parts[q][...], rows_of(got_ref, q, height))
            out_ref[at, :] = base_ref[at, :] - product(w, a_ref)

    pl.when(core_is(0))(functools.partial(run, True, own_ref))
    pl.when(core_is(1))(functools.partial(run, False, other_ref))


def write_kernel(masks, chosen, resume, a_ref, after_ref, got_ref, got_late_ref, *refs):
    count = len(masks)
    first, second = refs[:count], refs[count:2 * count]
    refs = refs[2 * count + (2 if resume else 0):]
    coef_ref, resid_ref, coefs, resids, sems = refs
    height = first[0].shape[0]
    places = spans(masks, 2 * height)

    def copies(k):
        at = places[chosen[k]]
        return (
            pltpu.make_async_copy(coefs.at[k], coef_ref.at[at, :], sems.at[0, k]),
            pltpu.make_async_copy(resids.at[k], resid_ref.at[at, :], sems.at[1, k]),
        )

    for k, q in enumerate(chosen):
        @pl.when(core_is(0))
        def _():
            w = both_panels(True, first[q][...], rows_of(got_ref, q, height))
            coefs[k] = w.astype(F32)
            resids[k] = after_ref[places[q], :]

        @pl.when(core_is(1))
        def _():
            w = both_panels(False, second[q][...], rows_of(got_late_ref, k, height))
            coefs[k] = w.astype(F32)
            resids[k] = after_ref[places[q], :] - product(w, a_ref)

        for copy in copies(k):
            copy.start()
    for k in range(len(chosen)):
        for copy in copies(k):
            copy.wait()


def write_call(masks, chosen, shapes, arrays, resume=()):
    height = 2 * arrays[4].shape[0]
    feats, rows = shapes[0].shape[1], shapes[1].shape[1]
    size = len(chosen)
    return pl.pallas_call(
        functools.partial(write_kernel, masks, chosen, len(resume) > 0),
        out_shape=shapes,
        in_specs=[VMEM] * len(arrays) + [ANY] * len(resume),
        out_specs=[ANY] * 2,
        scratch_shapes=[
            pltpu.VMEM((size, height, feats), F32),
            pltpu.VMEM((size, height, rows), F32),
            pltpu.SemaphoreType.DMA((2, size)),
        ],
        input_output_aliases={len(arrays) + k: k for k in range(len(resume))},
        compiler_params=pltpu.CompilerParams(vmem_limit_bytes=GRANT),
        name="write_rest" if resume else "write_early",
    )(*arrays, *resume)


def base_kernel(masks, turned_ref, got_ref, *refs):
    parts, out_ref = refs[:-1], refs[-1]
    height = parts[0].shape[0]
    first_plane = lax.axis_index("grp") < CORES

    @pl.when(first_plane)
    def _():
        out_ref[...] = turned_ref[...]

    def run(first_core):
        for q, at in enumerate(spans(masks, 2 * height)):
            r = both_panels(first_core, parts[q][...], rows_of(got_ref, q, height))
            out_ref[at, :] = r.astype(F32)

    later = jnp.logical_not(first_plane)
    pl.when(jnp.logical_and(later, core_is(0)))(functools.partial(run, True))
    pl.when(jnp.logical_and(later, core_is(1)))(functools.partial(run, False))


def local_call(body, out_shape, arrays):
    many = isinstance(out_shape, (list, tuple))
    return pl.pallas_call(
        body,
        out_shape=out_shape,
        in_specs=[VMEM] * len(arrays),
        out_specs=[VMEM] * len(out_shape) if many else VMEM,
        compiler_params=pltpu.CompilerParams(vmem_limit_bytes=GRANT),
    )(*arrays)


def first_call(owner, layout, panel, own, other):
    feats = own[0].shape[1]
    width, rows = panel.shape
    return pl.pallas_call(
        functools.partial(first_kernel, layout, owner),
        out_shape=jax.ShapeDtypeStruct((width, feats), BF16),
        in_specs=[VMEM] * (1 + 2 * len(own)),
        out_specs=VMEM,
        cost_estimate=pl.CostEstimate(
            flops=2 * width * rows * feats, bytes_accessed=2 * rows * feats, transcendentals=0
        ),
        compiler_params=pltpu.CompilerParams(vmem_limit_bytes=GRANT),
        name="first_corr",
    )(panel, *own, *other)


def stage_call(owner, layout, panel, ca, cb, squares, own, other, kind):
    feats = own[0].shape[1]
    width, rows = panel.shape
    out_shape = [jax.ShapeDtypeStruct((width, feats), BF16)]
    if kind is None:
        own, other, layout = [panel], [panel], [1]
    else:
        out_shape.append(jax.ShapeDtypeStruct(panel.shape, kind))
    return pl.pallas_call(
        functools.partial(stage_kernel, layout, owner),
        out_shape=out_shape,
        in_specs=[VMEM] * (5 + 2 * len(own)),
        out_specs=[VMEM] * len(out_shape),
        cost_estimate=pl.CostEstimate(
            flops=2 * width * feats * (2 * feats + rows),
            bytes_accessed=2 * feats * (feats + rows),
            transcendentals=0,
        ),
        compiler_params=pltpu.CompilerParams(vmem_limit_bytes=GRANT),
        name="sweep_stage",
    )(panel, ca, cb, *squares, *own, *other)


def sweep(features, residual, precond):
    grp_count, row_count = lax.axis_size("grp"), lax.axis_size("row")
    g, r = lax.axis_index("grp"), lax.axis_index("row")
    core = g % CORES
    plane = g // CORES
    plane_count = grp_count // CORES
    rows, feats = features.shape
    targets = residual.shape[1]
    panel_count = row_count // PAIR * CORES
    width = targets // panel_count

    def permute(x, mask=0, flip=0, keep=None, shift=0):
        route = []
        for a in range(grp_count):
            if keep is not None and a % CORES != keep:
                continue
            b = (a ^ flip) + shift
            if b >= grp_count:
                continue
            for i in range(row_count):
                route.append((a * row_count + i, b * row_count + (i ^ mask)))
        return lax.ppermute(x, ("grp", "row"), route)

    bits = [1 << i for i in range(row_count.bit_length() - 1) if (1 << i) != PAIR]
    masks = [0]
    for bit in reversed(bits):
        masks += [m ^ bit for m in masks]

    def after(x, *others):
        return lax.optimization_barrier((x,) + others)[0]

    ranks = jnp.stack([place_of(r ^ m) for m in masks])

    def ordered(parts):
        if CORES * width % TILE == 0:
            return parts
        stacked = jnp.take(jnp.stack(parts), jnp.argsort(ranks), axis=0)
        return [stacked[q] for q in range(len(parts))]

    starts = [((place_of(r ^ m) * CORES + core) * width).astype(jnp.uint32) for m in masks]
    on_first = core == 0
    at_plane = [plane == step for step in range(plane_count)]
    features, starts, on_first, at_plane = lax.optimization_barrier(
        (features, starts, on_first, at_plane)
    )
    far = bits[-1]
    near = bits[:-1]
    count = len(masks)
    edges = [feats * e // CUTS[-1] for e in CUTS]
    parts_of_a = [features[:, low:high] for low, high in zip(edges[:-1], edges[1:])]

    held = {0: [features]}
    held[far] = [permute(x, mask=far) for x in parts_of_a]
    for bit in reversed(near):
        for m in masks:
            if m not in held and (m ^ bit) in held and not m & far:
                held[m] = [permute(x, mask=bit) for x in held[m ^ bit]]
    swapped = permute(features, flip=1)
    square = after(precond, swapped).astype(BF16)
    squares = (square, permute(square, flip=1))

    turned = residual.T
    zero = jnp.uint32(0)

    def slice_for(k):
        return lax.dynamic_slice(turned, (starts[k], zero), (width, rows))

    slices = [slice_for(k).astype(BF16) if m else slice_for(k) for k, m in enumerate(masks)]
    moved = [permute(x, mask=m) for x, m in zip(slices, masks) if m]
    panel = jnp.concatenate([slices[0]] + [x.astype(F32) for x in moved], axis=1)

    held[far][0], squares = lax.optimization_barrier((held[far][0], squares))
    for bit in reversed(near):
        for m in masks:
            if m not in held and (m ^ bit) in held and m & far:
                held[m] = [permute(x, mask=bit) for x in held[m ^ bit]]
    got_blocks = {0: [swapped]}
    for m in masks[1:]:
        got_blocks[m] = [permute(x, flip=1) for x in held[m]]
    layout = [len(held[m]) for m in masks]
    mine = [x for m in masks for x in held[m]]
    theirs = [x for m in masks for x in got_blocks[m]]

    keep_first = keep_second = passed = blocks = None
    for step in range(plane_count):
        end = step + 1 == plane_count
        corr = first_call(0, layout, panel, mine, theirs)
        got = permute(corr, mask=PAIR)
        if end and passed is not None:
            blocks = [passed[:, k * rows:(k + 1) * rows] for k in range(count)]
            blocks = [permute(x, mask=m) if m else x for x, m in zip(blocks, masks)]
        w1, panel1 = stage_call(0, layout, panel, corr, got, squares, mine, theirs, F32)
        keep_first = w1 if keep_first is None else jnp.where(at_plane[step], w1, keep_first)
        corr = first_call(1, layout, panel1, mine, theirs)
        got = permute(corr, mask=PAIR)
        w2, *panel2 = stage_call(
            1, layout, panel1, corr, got, squares, mine, theirs, None if end else BF16
        )
        keep_second = w2 if keep_second is None else jnp.where(at_plane[step], w2, keep_second)
        if not end:
            panel = permute(panel2[0], shift=CORES)
            passed = panel if passed is None else jnp.where(at_plane[step + 1], panel, passed)

    def gather(kept, pieces):
        size = feats // pieces
        parts = {0: [kept]}
        parts[far] = [permute(kept[:, k * size:(k + 1) * size], mask=far) for k in range(pieces)]
        for bit in reversed(near):
            for m in list(parts):
                parts[m ^ bit] = [permute(x, mask=bit) for x in parts[m]]
        return [parts[m] for m in masks]

    def joined(parts):
        return ordered([x[0] if len(x) == 1 else jnp.concatenate(x, axis=1) for x in parts])

    first_parts = joined(gather(keep_first, FIRST_PIECES))
    second_pieces = gather(keep_second, LAST_PIECES)
    second_parts = joined(second_pieces)
    first_got = permute(jnp.concatenate(first_parts, axis=0), flip=1)
    early = max(count - 1, 1)
    got_early = permute(jnp.concatenate(second_parts[:early], axis=0), flip=1)
    whole = jax.ShapeDtypeStruct((targets, rows), F32)
    base = turned
    if blocks is not None:
        blocks = ordered(blocks)
        base_got = permute(jnp.concatenate(blocks, axis=0), flip=1)
        base = local_call(functools.partial(base_kernel, masks), whole, [turned, base_got] + blocks)
    after_first = local_call(
        functools.partial(update_kernel, masks),
        whole,
        [features, swapped, base, first_got] + first_parts,
    )
    if CORES * width % TILE:
        def assembled(parts, got):
            got = [got[q * width:(q + 1) * width] for q in range(len(parts))]
            pairs = [
                jnp.where(on_first, jnp.concatenate((x, y), axis=0), jnp.concatenate((y, x), axis=0))
                for x, y in zip(parts, got)
            ]
            return jnp.concatenate(pairs, axis=0)

        got_all = [got_early]
        if early < count:
            late = jnp.concatenate(second_parts[early:], axis=0)
            got_all.append(permute(late, flip=1))
        second = assembled(second_parts, jnp.concatenate(got_all, axis=0))
        coef_t = jnp.where(on_first, assembled(first_parts, first_got), second).astype(F32)
        change = product(second, features)
        return coef_t.T, jnp.where(on_first, after_first, after_first - change).T[None]
    shapes = [jax.ShapeDtypeStruct((targets, feats), F32), whole]
    parts = [features, after_first, first_got]
    known = second_parts[:early] + second_parts[:1] * (count - early)
    done = write_call(masks, tuple(range(early)), shapes, parts + [got_early] + first_parts + known)
    if early < count:
        got_late = jnp.concatenate([permute(x, flip=1) for x in second_pieces[-1]], axis=1)
        done = write_call(
            masks,
            tuple(range(early, count)),
            shapes,
            parts + [got_late] + first_parts + second_parts,
            done,
        )
    coef_t, resid_t = done
    return coef_t.T, resid_t.T[None]


def solution(mesh):
    placed = (P("row", "grp"), P("row", None), P("grp", None))

    return jax.shard_map(
        sweep,
        mesh=mesh,
        in_specs=placed,
        out_specs=(P("grp", None), P("grp", "row", None)),
        check_vma=False,
    )
```

```python
import functools

import jax
import jax.numpy as jnp
from jax import lax
from jax.experimental import pallas as pl
from jax.experimental.pallas import tpu as pltpu
from jax.sharding import PartitionSpec as P


F32 = jnp.float32
BF16 = jnp.bfloat16
CORES = 2
PAIR = 2
FIRST_PIECES, LAST_PIECES = 1, 2
CUTS = (0, 2, 4, 6, 8)
TILE = 8
ANY = pl.BlockSpec(memory_space=pl.ANY)
VMEM = pl.BlockSpec(memory_space=pltpu.VMEM)
GRANT = 24 * 1024 * 1024


def grouped(refs, layout):
    out, at = [], 0
    for size in layout:
        out.append(refs[at:at + size])
        at += size
    return out


def correlation(r_ref, blocks, c_ref):
    rows = blocks[0][0].shape[0]
    split = max(blocks, key=len)
    lhs = [r_ref[:, q * rows:(q + 1) * rows].astype(BF16) for q in range(len(blocks))]
    start = 0
    for k, piece in enumerate(split):
        span = pl.ds(start, piece.shape[1])
        total = None
        for x, block in zip(lhs, blocks):
            part = block[0][:, span] if len(block) == 1 else block[k][...]
            part = jnp.dot(x, part, preferred_element_type=F32)
            total = part if total is None else total + part
        c_ref[:, span] = total.astype(BF16)
        start += piece.shape[1]


def core_is(index):
    return lax.axis_index("grp") % CORES == index


def first_kernel(layout, owner, r_ref, *refs):
    count = sum(layout)

    @pl.when(core_is(owner))
    def _():
        correlation(r_ref, grouped(refs[:count], layout), refs[2 * count])

    @pl.when(core_is(1 - owner))
    def _():
        correlation(r_ref, grouped(refs[count:2 * count], layout), refs[2 * count])


def stage_kernel(layout, owner, r_ref, ca_ref, cb_ref, own_ref, other_ref, *refs):
    count = sum(layout)
    w_ref, rn_ref, next_ref = refs[2 * count], refs[2 * count + 1:2 * count + 2], refs[2 * count + 2:]
    width = ca_ref.shape[0]
    total = ca_ref[...].astype(F32) + cb_ref[...].astype(F32)
    high = total.astype(BF16)
    low = (total - high.astype(F32)).astype(BF16)
    stacked = jnp.concatenate((high, low), axis=0)

    def run(map_ref, blocks, nexts):
        both = jnp.dot(stacked, map_ref[...], preferred_element_type=F32)
        wb = (both[:width] + both[width:]).astype(BF16)
        w_ref[...] = wb
        if not rn_ref:
            return
        rows = blocks[0][0].shape[0]
        for q, block in enumerate(blocks):
            span = pl.ds(q * rows, rows)
            change, start = None, 0
            for piece in block:
                size = piece.shape[1]
                part = product(wb[:, start:start + size], piece)
                change = part if change is None else change + part
                start += size
            rn_ref[0][:, span] = (r_ref[:, span].astype(F32) - change).astype(rn_ref[0].dtype)
        if next_ref:
            correlation(rn_ref[0], nexts, next_ref[0])

    own, other = grouped(refs[:count], layout), grouped(refs[count:2 * count], layout)

    @pl.when(core_is(owner))
    def _():
        run(own_ref, own, other)

    @pl.when(core_is(1 - owner))
    def _():
        run(other_ref, other, own)


def product(w, a_ref):
    return lax.dot_general(w, a_ref[...], (((1,), (1,)), ((), ())), preferred_element_type=F32)


def place_of(index):
    return (index // (2 * PAIR)) * PAIR + index % PAIR


def spans(masks, height):
    if height % TILE:
        return [pl.ds(q * height, height) for q in range(len(masks))]
    shard = lax.axis_index("row")
    places = [place_of(lax.bitwise_xor(shard, jnp.int32(m))) for m in masks]
    return [pl.ds(pl.multiple_of(place * height, TILE), height) for place in places]


def rows_of(ref, q, height):
    return ref[q * height:(q + 1) * height, :]


def both_panels(first_core, own, got):
    return jnp.concatenate((own, got) if first_core else (got, own), axis=0)


def update_kernel(masks, own_ref, other_ref, base_ref, got_ref, *refs):
    parts, out_ref = refs[:-1], refs[-1]
    height = parts[0].shape[0]

    def run(first_core, a_ref):
        for q, at in enumerate(spans(masks, 2 * height)):
            w = both_panels(first_core, parts[q][...], rows_of(got_ref, q, height))
            out_ref[at, :] = base_ref[at, :] - product(w, a_ref)

    pl.when(core_is(0))(functools.partial(run, True, own_ref))
    pl.when(core_is(1))(functools.partial(run, False, other_ref))


def write_kernel(masks, chosen, resume, a_ref, after_ref, got_ref, got_late_ref, *refs):
    count = len(masks)
    first, second = refs[:count], refs[count:2 * count]
    refs = refs[2 * count + (2 if resume else 0):]
    coef_ref, resid_ref, coefs, resids, sems = refs
    height = first[0].shape[0]
    places = spans(masks, 2 * height)

    def copies(k):
        at = places[chosen[k]]
        return (
            pltpu.make_async_copy(coefs.at[k], coef_ref.at[at, :], sems.at[0, k]),
            pltpu.make_async_copy(resids.at[k], resid_ref.at[at, :], sems.at[1, k]),
        )

    for k, q in enumerate(chosen):
        @pl.when(core_is(0))
        def _():
            w = both_panels(True, first[q][...], rows_of(got_ref, q, height))
            coefs[k] = w.astype(F32)
            resids[k] = after_ref[places[q], :]

        @pl.when(core_is(1))
        def _():
            w = both_panels(False, second[q][...], rows_of(got_late_ref, k, height))
            coefs[k] = w.astype(F32)
            resids[k] = after_ref[places[q], :] - product(w, a_ref)

        for copy in copies(k):
            copy.start()
    for k in range(len(chosen)):
        for copy in copies(k):
            copy.wait()


def write_call(masks, chosen, shapes, arrays, resume=()):
    height = 2 * arrays[4].shape[0]
    feats, rows = shapes[0].shape[1], shapes[1].shape[1]
    size = len(chosen)
    return pl.pallas_call(
        functools.partial(write_kernel, masks, chosen, len(resume) > 0),
        out_shape=shapes,
        in_specs=[VMEM] * len(arrays) + [ANY] * len(resume),
        out_specs=[ANY] * 2,
        scratch_shapes=[
            pltpu.VMEM((size, height, feats), F32),
            pltpu.VMEM((size, height, rows), F32),
            pltpu.SemaphoreType.DMA((2, size)),
        ],
        input_output_aliases={len(arrays) + k: k for k in range(len(resume))},
        compiler_params=pltpu.CompilerParams(vmem_limit_bytes=GRANT),
        name="write_rest" if resume else "write_early",
    )(*arrays, *resume)


def base_kernel(masks, turned_ref, got_ref, *refs):
    parts, out_ref = refs[:-1], refs[-1]
    height = parts[0].shape[0]
    first_plane = lax.axis_index("grp") < CORES

    @pl.when(first_plane)
    def _():
        out_ref[...] = turned_ref[...]

    def run(first_core):
        for q, at in enumerate(spans(masks, 2 * height)):
            r = both_panels(first_core, parts[q][...], rows_of(got_ref, q, height))
            out_ref[at, :] = r.astype(F32)

    later = jnp.logical_not(first_plane)
    pl.when(jnp.logical_and(later, core_is(0)))(functools.partial(run, True))
    pl.when(jnp.logical_and(later, core_is(1)))(functools.partial(run, False))


def local_call(body, out_shape, arrays):
    many = isinstance(out_shape, (list, tuple))
    return pl.pallas_call(
        body,
        out_shape=out_shape,
        in_specs=[VMEM] * len(arrays),
        out_specs=[VMEM] * len(out_shape) if many else VMEM,
        compiler_params=pltpu.CompilerParams(vmem_limit_bytes=GRANT),
    )(*arrays)


def first_call(owner, layout, panel, own, other):
    feats = own[0].shape[1]
    width, rows = panel.shape
    return pl.pallas_call(
        functools.partial(first_kernel, layout, owner),
        out_shape=jax.ShapeDtypeStruct((width, feats), BF16),
        in_specs=[VMEM] * (1 + 2 * len(own)),
        out_specs=VMEM,
        cost_estimate=pl.CostEstimate(
            flops=2 * width * rows * feats, bytes_accessed=2 * rows * feats, transcendentals=0
        ),
        compiler_params=pltpu.CompilerParams(vmem_limit_bytes=GRANT),
        name="first_corr",
    )(panel, *own, *other)


def stage_call(owner, layout, panel, ca, cb, squares, own, other, kind):
    feats = own[0].shape[1]
    width, rows = panel.shape
    out_shape = [jax.ShapeDtypeStruct((width, feats), BF16)]
    if kind is None:
        own, other, layout = [panel], [panel], [1]
    else:
        out_shape.append(jax.ShapeDtypeStruct(panel.shape, kind))
    if kind == F32:
        out_shape.append(jax.ShapeDtypeStruct((width, feats), BF16))
    return pl.pallas_call(
        functools.partial(stage_kernel, layout, owner),
        out_shape=out_shape,
        in_specs=[VMEM] * (5 + 2 * len(own)),
        out_specs=[VMEM] * len(out_shape),
        cost_estimate=pl.CostEstimate(
            flops=2 * width * feats * (2 * feats + rows),
            bytes_accessed=2 * feats * (feats + rows),
            transcendentals=0,
        ),
        compiler_params=pltpu.CompilerParams(vmem_limit_bytes=GRANT),
        name="sweep_stage",
    )(panel, ca, cb, *squares, *own, *other)


def sweep(features, residual, precond):
    grp_count, row_count = lax.axis_size("grp"), lax.axis_size("row")
    g, r = lax.axis_index("grp"), lax.axis_index("row")
    core = g % CORES
    plane = g // CORES
    plane_count = grp_count // CORES
    rows, feats = features.shape
    targets = residual.shape[1]
    panel_count = row_count // PAIR * CORES
    width = targets // panel_count

    def permute(x, mask=0, flip=0, keep=None, shift=0):
        route = []
        for a in range(grp_count):
            if keep is not None and a % CORES != keep:
                continue
            b = (a ^ flip) + shift
            if b >= grp_count:
                continue
            for i in range(row_count):
                route.append((a * row_count + i, b * row_count + (i ^ mask)))
        return lax.ppermute(x, ("grp", "row"), route)

    bits = [1 << i for i in range(row_count.bit_length() - 1) if (1 << i) != PAIR]
    masks = [0]
    for bit in reversed(bits):
        masks += [m ^ bit for m in masks]

    def after(x, *others):
        return lax.optimization_barrier((x,) + others)[0]

    ranks = jnp.stack([place_of(r ^ m) for m in masks])

    def ordered(parts):
        if CORES * width % TILE == 0:
            return parts
        stacked = jnp.take(jnp.stack(parts), jnp.argsort(ranks), axis=0)
        return [stacked[q] for q in range(len(parts))]

    starts = [((place_of(r ^ m) * CORES + core) * width).astype(jnp.uint32) for m in masks]
    on_first = core == 0
    at_plane = [plane == step for step in range(plane_count)]
    features, starts, on_first, at_plane = lax.optimization_barrier(
        (features, starts, on_first, at_plane)
    )
    far = bits[-1]
    near = bits[:-1]
    count = len(masks)
    edges = [feats * e // CUTS[-1] for e in CUTS]
    parts_of_a = [features[:, :edges[1]]]
    again = after(features, parts_of_a[0])
    parts_of_a += [again[:, low:high] for low, high in zip(edges[1:-1], edges[2:])]

    held = {0: [features]}
    held[far] = [permute(x, mask=far) for x in parts_of_a]
    for bit in reversed(near):
        for m in masks:
            if m not in held and (m ^ bit) in held and not m & far:
                held[m] = [permute(x, mask=bit) for x in held[m ^ bit]]
    swapped = permute(features, flip=1)
    square = after(precond, swapped).astype(BF16)
    squares = (square, permute(square, flip=1))

    turned = residual.T
    zero = jnp.uint32(0)

    def slice_for(k):
        return lax.dynamic_slice(turned, (starts[k], zero), (width, rows))

    slices = [slice_for(k).astype(BF16) if m else slice_for(k) for k, m in enumerate(masks)]
    moved = [permute(x, mask=m) for x, m in zip(slices, masks) if m]
    panel = jnp.concatenate([slices[0]] + [x.astype(F32) for x in moved], axis=1)

    held[far][0], squares = lax.optimization_barrier((held[far][0], squares))
    for bit in reversed(near):
        for m in masks:
            if m not in held and (m ^ bit) in held and m & far:
                held[m] = [permute(x, mask=bit) for x in held[m ^ bit]]
    got_blocks = {0: [swapped]}
    for m in masks[1:]:
        got_blocks[m] = [permute(x, flip=1) for x in held[m]]
    layout = [len(held[m]) for m in masks]
    mine = [x for m in masks for x in held[m]]
    theirs = [x for m in masks for x in got_blocks[m]]

    keep_first = keep_second = passed = blocks = None
    for step in range(plane_count):
        end = step + 1 == plane_count
        corr = first_call(0, layout, panel, mine, theirs)
        got = permute(corr, mask=PAIR)
        if end and passed is not None:
            blocks = [passed[:, k * rows:(k + 1) * rows] for k in range(count)]
            blocks = [permute(x, mask=m) if m else x for x, m in zip(blocks, masks)]
        w1, panel1, corr = stage_call(0, layout, panel, corr, got, squares, mine, theirs, F32)
        keep_first = w1 if keep_first is None else jnp.where(at_plane[step], w1, keep_first)
        got = permute(corr, mask=PAIR)
        w2, *panel2 = stage_call(
            1, layout, panel1, corr, got, squares, mine, theirs, None if end else BF16
        )
        keep_second = w2 if keep_second is None else jnp.where(at_plane[step], w2, keep_second)
        if not end:
            panel = permute(panel2[0], shift=CORES)
            passed = panel if passed is None else jnp.where(at_plane[step + 1], panel, passed)

    def gather(kept, pieces):
        size = feats // pieces
        parts = {0: [kept]}
        parts[far] = [permute(kept[:, k * size:(k + 1) * size], mask=far) for k in range(pieces)]
        for bit in reversed(near):
            for m in list(parts):
                parts[m ^ bit] = [permute(x, mask=bit) for x in parts[m]]
        return [parts[m] for m in masks]

    def joined(parts):
        return ordered([x[0] if len(x) == 1 else jnp.concatenate(x, axis=1) for x in parts])

    first_parts = joined(gather(keep_first, FIRST_PIECES))
    second_pieces = gather(keep_second, LAST_PIECES)
    second_parts = joined(second_pieces)
    first_got = permute(jnp.concatenate(first_parts, axis=0), flip=1)
    early = max(count - 1, 1)
    got_early = permute(jnp.concatenate(second_parts[:early], axis=0), flip=1)
    whole = jax.ShapeDtypeStruct((targets, rows), F32)
    base = turned
    if blocks is not None:
        blocks = ordered(blocks)
        base_got = permute(jnp.concatenate(blocks, axis=0), flip=1)
        base = local_call(functools.partial(base_kernel, masks), whole, [turned, base_got] + blocks)
    after_first = local_call(
        functools.partial(update_kernel, masks),
        whole,
        [features, swapped, base, first_got] + first_parts,
    )
    if CORES * width % TILE:
        def assembled(parts, got):
            got = [got[q * width:(q + 1) * width] for q in range(len(parts))]
            pairs = [
                jnp.where(on_first, jnp.concatenate((x, y), axis=0), jnp.concatenate((y, x), axis=0))
                for x, y in zip(parts, got)
            ]
            return jnp.concatenate(pairs, axis=0)

        got_all = [got_early]
        if early < count:
            late = jnp.concatenate(second_parts[early:], axis=0)
            got_all.append(permute(late, flip=1))
        second = assembled(second_parts, jnp.concatenate(got_all, axis=0))
        coef_t = jnp.where(on_first, assembled(first_parts, first_got), second).astype(F32)
        change = product(second, features)
        return coef_t.T, jnp.where(on_first, after_first, after_first - change).T[None]
    shapes = [jax.ShapeDtypeStruct((targets, feats), F32), whole]
    parts = [features, after_first, first_got]
    known = second_parts[:early] + second_parts[:1] * (count - early)
    done = write_call(masks, tuple(range(early)), shapes, parts + [got_early] + first_parts + known)
    if early < count:
        got_late = jnp.concatenate([permute(x, flip=1) for x in second_pieces[-1]], axis=1)
        done = write_call(
            masks,
            tuple(range(early, count)),
            shapes,
            parts + [got_late] + first_parts + second_parts,
            done,
        )
    coef_t, resid_t = done
    return coef_t.T, resid_t.T[None]


def solution(mesh):
    placed = (P("row", "grp"), P("row", None), P("grp", None))

    return jax.shard_map(
        sweep,
        mesh=mesh,
        in_specs=placed,
        out_specs=(P("grp", None), P("grp", "row", None)),
        check_vma=False,
    )
```
